768 devices in a mesh: depth: 32 (over y, x), rows: 24 (over z, core).
Axes of the slice: x: 4, y: 8, z: 12, core: 2. Of those that a mesh axis runs over, the one named last changes fastest.
Arguments:
- volume: int32 [2, 256, 768, 1024], P(None, 'depth', 'rows'), may hold values from 0 to 255
- color_map: int32 [3, 256], replicated, may hold values from 0 to 255
- alpha_map: int32 [256], replicated, may hold values from 0 to 255
Outputs:
- image: float32 [4, 768, 1024], P(None, ('rows', 'depth'))
The draws below stay inside these ranges and needn't reach their ends.
All inputs are finite; a program needn't handle non-finite values.
Results may differ from the reference program's by a relative error of at most 0.003.
Values may be sent and summed in bfloat16 or wider, within the bound.
A program may use at most 64 MiB of HBM per device.

```python
import jax
import jax.numpy as jnp
from jax import lax

NZ = 1024
LEVELS = 256
NX = 256
NY = 768


def set_ends(values, key, least, top_value):
    dims = values.shape
    place = [jax.random.randint(jax.random.fold_in(key, axis), (), 0, dims[axis]) for axis in range(len(dims))]
    values = values.at[tuple(place)].set(least)
    longest = dims.index(max(dims))
    place[longest] = (place[longest] + 1) % dims[longest]
    return values.at[tuple(place)].set(top_value)


def setup_inputs(seed: int = 0) -> dict:
    arg_keys = jax.random.split(jax.random.key(seed), 4)
    return {
        "volume": set_ends(jax.random.randint(arg_keys[0], (2, NX, NY, NZ), 0, LEVELS), jax.random.fold_in(arg_keys[0], 1), 0, LEVELS - 1).astype(jnp.int32),
        "color_map": set_ends(jax.random.randint(arg_keys[1], (3, LEVELS), 0, 256), jax.random.fold_in(arg_keys[1], 1), 0, 255).astype(jnp.int32),
        "alpha_map": set_ends(jax.random.randint(arg_keys[2], (LEVELS,), 0, 256), jax.random.fold_in(arg_keys[2], 1), 0, 255).astype(jnp.int32),
    }


LIGHT_DEPTH = 0.48
LIGHT_ROWS = 0.6
LIGHT_COLS = 0.64
OPACITY = 4.0

def sample_slice(values, position):
    inside = (position >= 0) & (position < values.shape[0])
    clamped = jnp.clip(position, 0, values.shape[0] - 1).astype(jnp.int32)
    taken = lax.dynamic_index_in_dim(values, clamped, 0, keepdims=False)
    return jnp.where(inside, taken.astype(jnp.float32), jnp.float32(0.0))

def reference(volume, color_map, alpha_map):
    primary = volume[0]
    secondary = volume[1]
    color_table = color_map.astype(jnp.float32) / 255.0
    alpha_table = alpha_map.astype(jnp.float32) * (OPACITY / (255.0 * NX))

    def march_slice(running, position):
        color_sum, alpha_sum = running
        ahead = sample_slice(primary, position + 1)
        behind = sample_slice(primary, position - 1)
        current = sample_slice(primary, position)
        padded = jnp.pad(current, 1)
        grad_depth = 0.5 * (ahead - behind)
        grad_rows = 0.5 * (padded[2:, 1:-1] - padded[:-2, 1:-1])
        grad_cols = 0.5 * (padded[1:-1, 2:] - padded[1:-1, :-2])
        magnitude = jnp.sqrt(grad_depth * grad_depth + grad_rows * grad_rows + grad_cols * grad_cols)
        facing = LIGHT_DEPTH * grad_depth + LIGHT_ROWS * grad_rows + LIGHT_COLS * grad_cols
        shading = 0.3 + 0.7 * jnp.abs(facing) / jnp.maximum(magnitude, 1.0)
        primary_level = lax.dynamic_index_in_dim(primary, position, 0, keepdims=False)
        secondary_level = lax.dynamic_index_in_dim(secondary, position, 0, keepdims=False)
        emitted = jnp.take(color_table, primary_level, axis=1)
        opacity = jnp.take(alpha_table, secondary_level)
        weight = 1.0 - alpha_sum
        color_sum = color_sum + weight[None] * emitted * (opacity * shading)[None]
        alpha_sum = alpha_sum + weight * opacity
        return ((color_sum, alpha_sum), None)
    starting = (jnp.zeros((3, NY, NZ), jnp.float32), jnp.zeros((NY, NZ), jnp.float32))
    (color_sum, alpha_sum), _ = lax.scan(march_slice, starting, jnp.arange(NX, dtype=jnp.int32))
    return jnp.concatenate([color_sum, alpha_sum[None]], axis=0)
```

```python
import functools

import jax
import jax.numpy as jnp
from jax import lax
from jax.experimental import pallas as pl
from jax.experimental.pallas import tpu as pltpu
from jax.sharding import PartitionSpec as P

LIGHT_DEPTH = 0.336
LIGHT_ROWS = 0.42
LIGHT_COLS = 0.448
OPACITY = 4.0
LANES = 128
SUBS = 8
MESH = pl.DeviceIdType.MESH
F32 = jnp.float32


def take(table, index):
    return jnp.take_along_axis(table, index, axis=1, mode="promise_in_bounds")


def kernel(
    slices, height, depth_count, row_count,
    volume, color_ref, alpha_ref, out_ref,
    first, second, row_halo, depth_halo, part, sent, got,
    load_sem, halo_send, halo_recv, send_sem, recv_sem,
):
    S, H, D, R = slices, height, depth_count, row_count
    d, r = lax.axis_index("depth"), lax.axis_index("rows")

    loads = []
    for p, buffer in enumerate((first, second)):
        for block in range(SUBS):
            source = volume.at[p, :, :, pl.ds(block * LANES, LANES)]
            target = buffer.at[:, pl.ds(1, H), block, :] if p == 0 else buffer.at[:, :, block, :]
            load = pltpu.make_async_copy(source, target, load_sem.at[p, block])
            load.start()
            loads.append(load)

    barrier = pltpu.get_barrier_semaphore()

    def greet(k, _):
        pl.semaphore_signal(
            barrier, inc=1, device_id=(lax.rem(d + k, D), r), device_id_type=MESH
        )
        return 0

    lax.fori_loop(1, D, greet, 0)

    @pl.when(r > 0)
    def _():
        pl.semaphore_signal(barrier, inc=1, device_id=(d, r - 1), device_id_type=MESH)

    @pl.when(r < R - 1)
    def _():
        pl.semaphore_signal(barrier, inc=1, device_id=(d, r + 1), device_id_type=MESH)

    lane = lax.broadcasted_iota(jnp.int32, (SUBS, LANES), 1)
    sub = lax.broadcasted_iota(jnp.int32, (SUBS, LANES), 0)
    last_lane, first_lane = lane == LANES - 1, lane == 0
    not_last, not_first = (sub < SUBS - 1).astype(F32), (sub > 0).astype(F32)

    def spread(row):
        return jnp.broadcast_to(row, (SUBS, LANES))

    colors = color_ref[0:1] + color_ref[1:2] * 256 + color_ref[2:3] * 65536
    color_low, color_high = spread(colors[:, :LANES]), spread(colors[:, LANES:])
    alphas = spread(alpha_ref[0:1] + alpha_ref[1:2] * 256)

    zero = jnp.zeros((SUBS, LANES), jnp.int32)

    @pl.when(d == 0)
    def _():
        for i in range(H):
            depth_halo[0, i] = zero

    @pl.when(d == D - 1)
    def _():
        for i in range(H):
            depth_halo[1, i] = zero

    @pl.when(r == 0)
    def _():
        for s in range(S):
            row_halo[0, s] = zero

    @pl.when(r == R - 1)
    def _():
        for s in range(S):
            row_halo[1, s] = zero

    for load in loads[:SUBS]:
        load.wait()
    n_greet = D - 1 + (r > 0).astype(jnp.int32) + (r < R - 1).astype(jnp.int32)
    pl.semaphore_wait(barrier, n_greet)

    def halo(which, source, target, device):
        return pltpu.make_async_remote_copy(
            src_ref=source, dst_ref=target, send_sem=halo_send.at[which],
            recv_sem=halo_recv.at[which], device_id=device, device_id_type=MESH,
        )

    own = pl.ds(1, H)
    ahead = halo(0, first.at[S - 1, own], depth_halo.at[0], (d + 1, r))
    behind = halo(1, first.at[0, own], depth_halo.at[1], (d - 1, r))
    below = halo(2, first.at[:, H], row_halo.at[0], (d, r + 1))
    above = halo(3, first.at[:, 1], row_halo.at[1], (d, r - 1))
    halos = (
        (ahead, d < D - 1, d > 0), (behind, d > 0, d < D - 1),
        (below, r < R - 1, r > 0), (above, r > 0, r < R - 1),
    )
    for copy, sends, _ in halos:
        @pl.when(sends)
        def _(copy=copy):
            copy.start()

    for load in loads[SUBS:]:
        load.wait()

    def inner(row):
        clear = jnp.ones((SUBS, LANES), F32)
        total = [jnp.zeros((SUBS, LANES), F32)] * 3
        value = [first[s, row + 1] for s in range(S)]
        for s in range(S):
            level = second[s, row]
            code = take(alphas, level & 127)
            opacity = ((code >> ((level >> 4) & 8)) & 255).astype(F32) * (OPACITY / (255.0 * S * D))
            index = value[s] & 127
            code = jnp.where(value[s] >= 128, take(color_high, index), take(color_low, index))
            emitted = [(code & 255).astype(F32), ((code >> 8) & 255).astype(F32), (code >> 16).astype(F32)]
            here = value[s].astype(F32)
            right = pltpu.roll(here, LANES - 1, 1)
            left = pltpu.roll(here, 1, 1)
            right = jnp.where(last_lane, pltpu.roll(right, SUBS - 1, 0) * not_last, right)
            left = jnp.where(first_lane, pltpu.roll(left, 1, 0) * not_first, left)
            grad_cols = right - left
            grad_rows = (first[s, row + 2] - first[s, row]).astype(F32)
            facing = LIGHT_ROWS * grad_rows + LIGHT_COLS * grad_cols
            square = grad_rows * grad_rows + grad_cols * grad_cols
            weight = clear * opacity
            clear = clear - weight
            weight = weight * (1.0 / 255.0)
            if 0 < s < S - 1:
                grad_depth = (value[s + 1] - value[s - 1]).astype(F32)
                facing = facing + LIGHT_DEPTH * grad_depth
                square = square + grad_depth * grad_depth
                lit = weight * (0.3 + jnp.abs(facing) * lax.rsqrt(jnp.maximum(square, 4.0)))
                total = [t + e * lit for t, e in zip(total, emitted)]
            else:
                for i, x in enumerate([weight, facing, square] + emitted):
                    part[row, (4 if s == 0 else 10) + i] = x
        for i, x in enumerate(total + [1.0 - clear]):
            part[row, i] = x

    def inner_pair(i, _):
        inner(2 * i + 1)
        inner(2 * i + 2)
        return 0

    lax.fori_loop(0, (H - 2) // 2, inner_pair, 0)

    for copy, _, receives in halos[2:]:
        @pl.when(receives)
        def _(copy=copy):
            copy.wait_recv()
    for s in range(S):
        first[s, 0] = row_halo[0, s]
        first[s, H + 1] = row_halo[1, s]

    def inner_edge(i, _):
        inner(i * (H - 1))
        return 0

    lax.fori_loop(0, 2, inner_edge, 0)

    for copy, _, receives in halos[:2]:
        @pl.when(receives)
        def _(copy=copy):
            copy.wait_recv()

    def outer(row, buffer, slot):
        total = [part[row, i] for i in range(3)]
        for at, grad in (
            (4, first[1, row + 1] - depth_halo[0, row]),
            (10, depth_halo[1, row] - first[S - 2, row + 1]),
        ):
            grad = grad.astype(F32)
            facing = part[row, at + 1] + LIGHT_DEPTH * grad
            square = part[row, at + 2] + grad * grad
            lit = part[row, at] * (0.3 + jnp.abs(facing) * lax.rsqrt(jnp.maximum(square, 4.0)))
            total = [t + part[row, at + 3 + i] * lit for i, t in enumerate(total)]
        total.append(part[row, 3])
        for i in range(2):
            pair = jnp.concatenate(total[2 * i : 2 * i + 2], axis=0)
            buffer[slot, pl.ds(16 * i, 16)] = pair.astype(jnp.bfloat16)

    def shipment(row):
        return pltpu.make_async_remote_copy(
            src_ref=sent.at[row], dst_ref=got.at[d], send_sem=send_sem.at[row],
            recv_sem=recv_sem.at[d], device_id=(row, r), device_id_type=MESH,
        )

    def ship(k, _):
        row = lax.rem(d + k, D)
        outer(row, sent, row)
        shipment(row).start()
        return 0

    lax.fori_loop(1, D, ship, 0)
    outer(d, got, d)

    def arrive(k, _):
        peer = lax.rem(d + k, D)
        pltpu.make_async_remote_copy(
            src_ref=sent.at[peer], dst_ref=got.at[peer], send_sem=send_sem.at[peer],
            recv_sem=recv_sem.at[peer], device_id=(peer, r), device_id_type=MESH,
        ).wait_recv()
        return 0

    lax.fori_loop(1, D, arrive, 0)

    clear = jnp.ones((SUBS, LANES), F32)
    total = [jnp.zeros((SUBS, LANES), F32)] * 3
    for k in range(D):
        slab = got[k].astype(F32)
        total = [t + clear * slab[SUBS * i : SUBS * (i + 1)] for i, t in enumerate(total)]
        clear = clear - clear * slab[3 * SUBS :]
    for i, x in enumerate(total + [1.0 - clear]):
        out_ref[i] = x

    def drain(k, _):
        shipment(lax.rem(d + k, D)).wait_send()
        return 0

    lax.fori_loop(1, D, drain, 0)
    for copy, sends, _ in halos:
        @pl.when(sends)
        def _(copy=copy):
            copy.wait_send()


def body(volume, color_map, alpha_map):
    D, R = lax.axis_size("depth"), lax.axis_size("rows")
    S, H = volume.shape[1], volume.shape[2]
    vmem = pl.BlockSpec(memory_space=pltpu.VMEM)
    image = pl.pallas_call(
        functools.partial(kernel, S, H, D, R),
        out_shape=jax.ShapeDtypeStruct((4, SUBS, LANES), F32),
        in_specs=[pl.BlockSpec(memory_space=pl.ANY), vmem, vmem],
        out_specs=vmem,
        scratch_shapes=[
            pltpu.VMEM((S, H + 2, SUBS, LANES), jnp.int32),
            pltpu.VMEM((S, H, SUBS, LANES), jnp.int32),
            pltpu.VMEM((2, S, SUBS, LANES), jnp.int32),
            pltpu.VMEM((2, H, SUBS, LANES), jnp.int32),
            pltpu.VMEM((H, 16, SUBS, LANES), F32),
            pltpu.VMEM((D, 4 * SUBS, LANES), jnp.bfloat16),
            pltpu.VMEM((D, 4 * SUBS, LANES), jnp.bfloat16),
            pltpu.SemaphoreType.DMA((2, SUBS)),
            pltpu.SemaphoreType.DMA((4,)),
            pltpu.SemaphoreType.DMA((4,)),
            pltpu.SemaphoreType.DMA((D,)),
            pltpu.SemaphoreType.DMA((D,)),
        ],
        compiler_params=pltpu.CompilerParams(collective_id=0, has_side_effects=True),
        name="render",
    )(volume, color_map, alpha_map.reshape(2, LANES))
    return image.reshape(4, 1, SUBS * LANES)


def solution(mesh):
    in_specs = (P(None, "depth", "rows", None), P(), P())
    out_specs = P(None, ("rows", "depth"), None)
    return jax.shard_map(body, mesh=mesh, in_specs=in_specs, out_specs=out_specs, check_vma=False)
```

```python
import functools

import jax
import jax.numpy as jnp
from jax import lax
from jax.experimental import pallas as pl
from jax.experimental.pallas import tpu as pltpu
from jax.sharding import PartitionSpec as P

LIGHT_DEPTH = 0.336
LIGHT_ROWS = 0.42
LIGHT_COLS = 0.448
OPACITY = 4.0
LANES = 128
SUBS = 8
MESH = pl.DeviceIdType.MESH
F32 = jnp.float32
X = 4
UNROLL = 5


def take(table, index):
    return jnp.take_along_axis(table, index, axis=1, mode="promise_in_bounds")


def kernel(
    slices, height, depth_count, row_count,
    volume, color_ref, alpha_ref, out_ref,
    first, second, row_halo, depth_edge, depth_halo, part, sent, got,
    load_sem, halo_send, halo_recv, send_sem, recv_sem, near_sem, far_sem,
):
    S, H, D, R = slices, height, depth_count, row_count
    d, r = lax.axis_index("depth"), lax.axis_index("rows")

    Y = D // X
    y, x = lax.div(d, X), lax.rem(d, X)
    HALF = H // 2

    def along(step):
        return lax.rem(y + step + Y, Y) * X + x

    barrier = pltpu.get_barrier_semaphore()

    def greet(device):
        pl.semaphore_signal(barrier, inc=1, device_id=device, device_id_type=MESH)

    def greet_if(condition, device):
        @pl.when(condition)
        def _():
            greet(device)

    crosses_up, crosses_down = (x == X - 1) & (d < D - 1), (x == 0) & (d > 0)
    greet_if(crosses_up, (d + 1, r))
    greet_if(crosses_down, (d - 1, r))
    for k in range(1, X):
        greet((y * X + lax.rem(x + k, X), r))
    for step in (1, -1, 2, -2):
        greet((along(step), r))
    greet_if(r > 0, (d, r - 1))
    greet_if(r < R - 1, (d, r + 1))
    n_greet = X + 3
    for condition in (crosses_up, crosses_down, r > 0, r < R - 1):
        n_greet = n_greet + condition.astype(jnp.int32)

    loads = []
    for p, buffer in enumerate((first, second)):
        for block in range(SUBS):
            source = volume.at[p, :, :, pl.ds(block * LANES, LANES)]
            target = buffer.at[:, pl.ds(1, H), block, :] if p == 0 else buffer.at[:, :, block, :]
            load = pltpu.make_async_copy(source, target, load_sem.at[p, block])
            load.start()
            loads.append(load)

    lane = lax.broadcasted_iota(jnp.int32, (SUBS, LANES), 1)
    sub = lax.broadcasted_iota(jnp.int32, (SUBS, LANES), 0)
    last_lane, first_lane = lane == LANES - 1, lane == 0
    not_last, not_first = (sub < SUBS - 1).astype(F32), (sub > 0).astype(F32)

    def spread(row):
        return jnp.broadcast_to(row, (SUBS, LANES))

    colors = color_ref[0:1] + color_ref[1:2] * 256 + color_ref[2:3] * 65536
    color_low, color_high = spread(colors[:, :LANES]), spread(colors[:, LANES:])
    alphas = spread(alpha_ref[0:1] + alpha_ref[1:2] * 256)

    zero = jnp.zeros((SUBS, LANES), jnp.int32)

    @pl.when(d == 0)
    def _():
        for i in range(HALF):
            depth_halo[0, i] = zero

    @pl.when(d == D - 1)
    def _():
        for i in range(HALF):
            depth_halo[1, i] = zero

    @pl.when(r == 0)
    def _():
        for s in range(S):
            row_halo[0, s] = zero

    @pl.when(r == R - 1)
    def _():
        for s in range(S):
            row_halo[1, s] = zero

    for load in loads[:SUBS]:
        load.wait()
    for i in range(HALF):
        depth_edge[0, i] = first[S - 1, i + 1] + first[S - 1, i + 1 + HALF] * 65536
        depth_edge[1, i] = first[0, i + 1] + first[0, i + 1 + HALF] * 65536
    pl.semaphore_wait(barrier, n_greet)

    def halo(which, source, target, device):
        return pltpu.make_async_remote_copy(
            src_ref=source, dst_ref=target, send_sem=halo_send.at[which],
            recv_sem=halo_recv.at[which], device_id=device, device_id_type=MESH,
        )

    ahead = halo(0, depth_edge.at[0], depth_halo.at[0], (d + 1, r))
    behind = halo(1, depth_edge.at[1], depth_halo.at[1], (d - 1, r))
    below = halo(2, first.at[:, H], row_halo.at[0], (d, r + 1))
    above = halo(3, first.at[:, 1], row_halo.at[1], (d, r - 1))
    halos = (
        (ahead, d < D - 1, d > 0), (behind, d > 0, d < D - 1),
        (below, r < R - 1, r > 0), (above, r > 0, r < R - 1),
    )
    for copy, sends, _ in halos:
        @pl.when(sends)
        def _(copy=copy):
            copy.start()

    for slot, side in ((1, 1), (0, -1)):
        for hops in (1, 2):
            pl.semaphore_signal(
                near_sem.at[slot, hops - 1], inc=1,
                device_id=(along(side * hops), r), device_id_type=MESH,
            )
    side = jnp.where(y <= Y // 2, 1, -1)
    middle = (y == 0) | ((y >= Y // 2 - 1) & (y <= Y // 2 + 1))

    def slot_of(side):
        return lax.div(1 - side, 2)

    def hear_near(side):
        pl.semaphore_wait(near_sem.at[slot_of(side), 0], 1)
        pl.semaphore_wait(near_sem.at[slot_of(side), 1], 1)
        pl.semaphore_signal(
            far_sem.at[slot_of(side)], inc=1, device_id=(along(-2 * side), r), device_id_type=MESH
        )

    for load in loads[SUBS:]:
        load.wait()

    def inner(row):
        clear = jnp.ones((SUBS, LANES), F32)
        total = [jnp.zeros((SUBS, LANES), F32)] * 3
        value = [first[s, row + 1] for s in range(S)]
        for s in range(S):
            level = second[s, row]
            code = take(alphas, level & 127)
            opacity = ((code >> ((level >> 4) & 8)) & 255).astype(F32) * (OPACITY / (255.0 * S * D))
            index = value[s] & 127
            code = jnp.where(value[s] >= 128, take(color_high, index), take(color_low, index))
            emitted = [(code & 255).astype(F32), ((code >> 8) & 255).astype(F32), (code >> 16).astype(F32)]
            here = value[s].astype(F32)
            right = pltpu.roll(here, LANES - 1, 1)
            left = pltpu.roll(here, 1, 1)
            right = jnp.where(last_lane, pltpu.roll(right, SUBS - 1, 0) * not_last, right)
            left = jnp.where(first_lane, pltpu.roll(left, 1, 0) * not_first, left)
            grad_cols = right - left
            grad_rows = (first[s, row + 2] - first[s, row]).astype(F32)
            facing = LIGHT_ROWS * grad_rows + LIGHT_COLS * grad_cols
            square = grad_rows * grad_rows + grad_cols * grad_cols
            weight = clear * opacity
            clear = clear - weight
            weight = weight * (1.0 / 255.0)
            if 0 < s < S - 1:
                grad_depth = (value[s + 1] - value[s - 1]).astype(F32)
                facing = facing + LIGHT_DEPTH * grad_depth
                square = square + grad_depth * grad_depth
                lit = weight * (0.3 + jnp.abs(facing) * lax.rsqrt(jnp.maximum(square, 4.0)))
                total = [t + e * lit for t, e in zip(total, emitted)]
            else:
                for i, x in enumerate([weight, facing, square] + emitted):
                    part[row, (4 if s == 0 else 10) + i] = x
        for i, x in enumerate(total + [1.0 - clear]):
            part[row, i] = x

    def inner_group(i, _):
        for k in range(UNROLL):
            inner(UNROLL * i + 1 + k)
        return 0

    groups = (H - 2) // UNROLL
    lax.fori_loop(0, groups // 2, inner_group, 0)
    hear_near(side)

    @pl.when(middle)
    def _():
        hear_near(-side)

    lax.fori_loop(groups // 2, groups, inner_group, 0)

    for copy, _, receives in halos[2:]:
        @pl.when(receives)
        def _(copy=copy):
            copy.wait_recv()
    for s in range(S):
        first[s, 0] = row_halo[0, s]
        first[s, H + 1] = row_halo[1, s]

    for row in (0, H - 1):
        inner(row)

    for copy, _, receives in halos[:2]:
        @pl.when(receives)
        def _(copy=copy):
            copy.wait_recv()

    def outer(row, buffer, slot):
        total = [part[row, i] for i in range(3)]
        word, shift = lax.rem(row, HALF), lax.div(row, HALF) * 16
        front, back = ((depth_halo[i, word] >> shift) & 255 for i in range(2))
        for at, grad in (
            (4, first[1, row + 1] - front),
            (10, back - first[S - 2, row + 1]),
        ):
            grad = grad.astype(F32)
            facing = part[row, at + 1] + LIGHT_DEPTH * grad
            square = part[row, at + 2] + grad * grad
            lit = part[row, at] * (0.3 + jnp.abs(facing) * lax.rsqrt(jnp.maximum(square, 4.0)))
            total = [t + part[row, at + 3 + i] * lit for i, t in enumerate(total)]
        total.append(part[row, 3])
        for i in range(2):
            pair = jnp.concatenate(total[2 * i : 2 * i + 2], axis=0)
            buffer[slot, pl.ds(16 * i, 16)] = pair.astype(jnp.bfloat16)

    def shipment(row):
        return pltpu.make_async_remote_copy(
            src_ref=sent.at[row], dst_ref=got.at[d], send_sem=send_sem.at[row],
            recv_sem=recv_sem.at[d], device_id=(row, r), device_id_type=MESH,
        )

    outer(d, got, d)
    for k in range(1, X):
        row = y * X + lax.rem(x + k, X)
        outer(row, sent, row)
        shipment(row).start()

    def ship(k, _):
        late = jnp.where(k < 4, k + 2, jnp.where(k < 6, k - 4, k))
        step = jnp.where(y == Y // 2, late, k)

        @pl.when(step == 0)
        def _():
            pl.semaphore_wait(far_sem.at[slot_of(side)], 1)

        @pl.when((step == 4) & jnp.logical_not(middle))
        def _():
            hear_near(-side)

        @pl.when(step == 6)
        def _():
            pl.semaphore_wait(far_sem.at[slot_of(-side)], 1)

        away = jnp.where(step < 2, step + 3, jnp.where(step < 4, step - 1, 3 - step))
        base = lax.rem(y + away * side + Y, Y) * X
        for i in range(X):
            outer(base + i, sent, base + i)
        for i in range(X):
            shipment(base + i).start()
        return 0

    lax.fori_loop(0, Y - 1, ship, 0)

    def arrive(k, _):
        peer = lax.rem(d + k, D)
        pltpu.make_async_remote_copy(
            src_ref=sent.at[peer], dst_ref=got.at[peer], send_sem=send_sem.at[peer],
            recv_sem=recv_sem.at[peer], device_id=(peer, r), device_id_type=MESH,
        ).wait_recv()
        return 0

    lax.fori_loop(1, D, arrive, 0)

    clear = jnp.ones((SUBS, LANES), F32)
    total = [jnp.zeros((SUBS, LANES), F32)] * 3
    for k in range(D):
        slab = got[k].astype(F32)
        total = [t + clear * slab[SUBS * i : SUBS * (i + 1)] for i, t in enumerate(total)]
        clear = clear - clear * slab[3 * SUBS :]
    for i, x in enumerate(total + [1.0 - clear]):
        out_ref[i] = x

    def drain(k, _):
        shipment(lax.rem(d + k, D)).wait_send()
        return 0

    lax.fori_loop(1, D, drain, 0)
    for copy, sends, _ in halos:
        @pl.when(sends)
        def _(copy=copy):
            copy.wait_send()


def body(volume, color_map, alpha_map):
    D, R = lax.axis_size("depth"), lax.axis_size("rows")
    S, H = volume.shape[1], volume.shape[2]
    vmem = pl.BlockSpec(memory_space=pltpu.VMEM)
    image = pl.pallas_call(
        functools.partial(kernel, S, H, D, R),
        out_shape=pltpu.VMEM((4, SUBS, LANES), F32),
        in_specs=[pl.BlockSpec(memory_space=pl.ANY), vmem, vmem],
        out_specs=vmem,
        scratch_shapes=[
            pltpu.VMEM((S, H + 2, SUBS, LANES), jnp.int32),
            pltpu.VMEM((S, H, SUBS, LANES), jnp.int32),
            pltpu.VMEM((2, S, SUBS, LANES), jnp.int32),
            pltpu.VMEM((2, H // 2, SUBS, LANES), jnp.int32),
            pltpu.VMEM((2, H // 2, SUBS, LANES), jnp.int32),
            pltpu.VMEM((H, 16, SUBS, LANES), F32),
            pltpu.VMEM((D, 4 * SUBS, LANES), jnp.bfloat16),
            pltpu.VMEM((D, 4 * SUBS, LANES), jnp.bfloat16),
            pltpu.SemaphoreType.DMA((2, SUBS)),
            pltpu.SemaphoreType.DMA((4,)),
            pltpu.SemaphoreType.DMA((4,)),
            pltpu.SemaphoreType.DMA((D,)),
            pltpu.SemaphoreType.DMA((D,)),
            pltpu.SemaphoreType.REGULAR((2, 2)),
            pltpu.SemaphoreType.REGULAR((2,)),
        ],
        compiler_params=pltpu.CompilerParams(collective_id=0, has_side_effects=True),
        name="render",
    )(volume, color_map, alpha_map.reshape(2, LANES))
    return image.reshape(4, 1, SUBS * LANES)


def solution(mesh):
    in_specs = (P(None, "depth", "rows", None), P(), P())
    out_specs = P(None, ("rows", "depth"), None)
    return jax.shard_map(body, mesh=mesh, in_specs=in_specs, out_specs=out_specs, check_vma=False)
```

```python
import functools

import jax
import jax.numpy as jnp
from jax import lax
from jax.experimental import pallas as pl
from jax.experimental.pallas import tpu as pltpu
from jax.sharding import PartitionSpec as P

LIGHT_DEPTH = 0.336
LIGHT_ROWS = 0.42
LIGHT_COLS = 0.448
OPACITY = 4.0
LANES = 128
SUBS = 8
MESH = pl.DeviceIdType.MESH
F32 = jnp.float32
X = 4
UNROLL = 5


def take(table, index):
    return jnp.take_along_axis(table, index, axis=1, mode="promise_in_bounds")


def kernel(
    slices, height, depth_count, row_count,
    volume, color_map, alpha_map, out_ref,
    color_ref, alpha_ref, first, second, row_halo, depth_edge, depth_halo, part, sent, got, joined, met,
    table_sem, load_sem, halo_send, halo_recv, sent_sem, got_sem, joined_sem, met_sem, news_sem, here_sem,
):
    S, H, D, R = slices, height, depth_count, row_count
    d, r = lax.axis_index("depth"), lax.axis_index("rows")

    Y = D // X
    y, x = lax.div(d, X), lax.rem(d, X)
    HALF = H // 2

    def along(step):
        return lax.rem(y + step + Y, Y) * X + x

    barrier = pltpu.get_barrier_semaphore()

    def greet(device):
        pl.semaphore_signal(barrier, inc=1, device_id=device, device_id_type=MESH)

    def greet_if(condition, device):
        @pl.when(condition)
        def _():
            greet(device)

    root = d == 0
    crosses_up, crosses_down = (x == X - 1) & (d < D - 1), (x == 0) & (d > 0)
    greet_if(crosses_up, (d + 1, r))
    greet_if(crosses_down, (d - 1, r))
    greet_if(root, (d + 1, r))

    @pl.when(jnp.logical_not(root))
    def _():
        for k in range(1, X):
            greet((y * X + lax.rem(x + k, X), r))
        for step in (1, -1, 2, -2):
            greet((along(step), r))

    greet_if(r > 0, (d, r - 1))
    greet_if(r < R - 1, (d, r + 1))
    greet_if((x == 0) & (y > 2) & (y < Y - 2), (0, r))
    hears_across = (y == 0) & (x > 1)
    hears_along = (x == 0) & (y > 0)
    beside_root = (x == 0) & ((y == 1) | (y == 2) | (y == Y - 1) | (y == Y - 2))
    n_greet = jnp.where(root, X + Y - 2, X + 3 - (hears_across | beside_root).astype(jnp.int32))
    for condition in (crosses_up, crosses_down, r > 0, r < R - 1):
        n_greet = n_greet + condition.astype(jnp.int32)

    tables = [
        pltpu.make_async_copy(color_map, color_ref, table_sem.at[0]),
        pltpu.make_async_copy(alpha_map, alpha_ref, table_sem.at[1]),
    ]
    loads = []
    for p, buffer in enumerate((first, second)):
        for block in range(SUBS):
            source = volume.at[p, :, :, pl.ds(block * LANES, LANES)]
            target = buffer.at[:, pl.ds(1, H), block, :] if p == 0 else buffer.at[:, :, block, :]
            load = pltpu.make_async_copy(source, target, load_sem.at[p, block])
            load.start()
            loads.append(load)
    for table in tables:
        table.start()

    lane = lax.broadcasted_iota(jnp.int32, (SUBS, LANES), 1)
    sub = lax.broadcasted_iota(jnp.int32, (SUBS, LANES), 0)
    last_lane, first_lane = lane == LANES - 1, lane == 0
    not_last, not_first = (sub < SUBS - 1).astype(F32), (sub > 0).astype(F32)

    def spread(row):
        return jnp.broadcast_to(row, (SUBS, LANES))

    zero = jnp.zeros((SUBS, LANES), jnp.int32)

    @pl.when(d == 0)
    def _():
        for i in range(HALF):
            depth_halo[0, i] = zero

    @pl.when(d == D - 1)
    def _():
        for i in range(HALF):
            depth_halo[1, i] = zero

    @pl.when(r == 0)
    def _():
        for s in range(S):
            row_halo[0, s] = zero

    @pl.when(r == R - 1)
    def _():
        for s in range(S):
            row_halo[1, s] = zero

    for load in loads[:SUBS]:
        load.wait()
    for i in range(HALF):
        depth_edge[0, i] = first[S - 1, i + 1] + first[S - 1, i + 1 + HALF] * 65536
        depth_edge[1, i] = first[0, i + 1] + first[0, i + 1 + HALF] * 65536
    pl.semaphore_wait(barrier, n_greet)

    def halo(which, source, target, device):
        return pltpu.make_async_remote_copy(
            src_ref=source, dst_ref=target, send_sem=halo_send.at[which],
            recv_sem=halo_recv.at[which], device_id=device, device_id_type=MESH,
        )

    ahead = halo(0, depth_edge.at[0], depth_halo.at[0], (d + 1, r))
    behind = halo(1, depth_edge.at[1], depth_halo.at[1], (d - 1, r))
    below = halo(2, first.at[:, H], row_halo.at[0], (d, r + 1))
    above = halo(3, first.at[:, 1], row_halo.at[1], (d, r - 1))
    halos = (
        (ahead, d < D - 1, d > 0), (behind, d > 0, d < D - 1),
        (below, r < R - 1, r > 0), (above, r > 0, r < R - 1),
    )
    for copy, sends, _ in halos:
        @pl.when(sends)
        def _(copy=copy):
            copy.start()

    def tell(semaphore, device):
        pl.semaphore_signal(semaphore, inc=1, device_id=device, device_id_type=MESH)

    @pl.when(root)
    def _():
        for k in range(2, X):
            tell(here_sem, (k, r))
        for k in range(1, Y):
            tell(here_sem, (k * X, r))

    for step in (2, -2):
        @pl.when(jnp.logical_not(root) & (along(step) != 0))
        def _(step=step):
            tell(news_sem, (along(step), r))

    @pl.when((x == 0) & (y == 1))
    def _():
        tell(news_sem, (along(1), r))

    @pl.when((x == 0) & (y == Y - 1))
    def _():
        tell(news_sem, (along(-1), r))

    for load in tables + loads[SUBS:]:
        load.wait()
    colors = color_ref[0:1] + color_ref[1:2] * 256 + color_ref[2:3] * 65536
    color_low, color_high = spread(colors[:, :LANES]), spread(colors[:, LANES:])
    alphas = spread(alpha_ref[0:1] + alpha_ref[1:2] * 256)

    def inner(row):
        clear = jnp.ones((SUBS, LANES), F32)
        total = [jnp.zeros((SUBS, LANES), F32)] * 3
        value = [first[s, row + 1] for s in range(S)]
        for s in range(S):
            level = second[s, row]
            code = take(alphas, level & 127)
            opacity = ((code >> ((level >> 4) & 8)) & 255).astype(F32) * (OPACITY / (255.0 * S * D))
            index = value[s] & 127
            code = jnp.where(value[s] >= 128, take(color_high, index), take(color_low, index))
            emitted = [(code & 255).astype(F32), ((code >> 8) & 255).astype(F32), (code >> 16).astype(F32)]
            here = value[s].astype(F32)
            right = pltpu.roll(here, LANES - 1, 1)
            left = pltpu.roll(here, 1, 1)
            right = jnp.where(last_lane, pltpu.roll(right, SUBS - 1, 0) * not_last, right)
            left = jnp.where(first_lane, pltpu.roll(left, 1, 0) * not_first, left)
            grad_cols = right - left
            grad_rows = (first[s, row + 2] - first[s, row]).astype(F32)
            facing = LIGHT_ROWS * grad_rows + LIGHT_COLS * grad_cols
            square = grad_rows * grad_rows + grad_cols * grad_cols
            weight = clear * opacity
            clear = clear - weight
            weight = weight * (1.0 / 255.0)
            if 0 < s < S - 1:
                grad_depth = (value[s + 1] - value[s - 1]).astype(F32)
                facing = facing + LIGHT_DEPTH * grad_depth
                square = square + grad_depth * grad_depth
                lit = weight * (0.3 + jnp.abs(facing) * lax.rsqrt(jnp.maximum(square, 4.0)))
                total = [t + e * lit for t, e in zip(total, emitted)]
            else:
                for i, x in enumerate([weight, facing, square] + emitted):
                    part[row, (4 if s == 0 else 10) + i] = x
        for i, x in enumerate(total + [1.0 - clear]):
            part[row, i] = x

    def inner_group(i, _):
        for k in range(UNROLL):
            inner(UNROLL * i + 1 + k)
        return 0

    lax.fori_loop(0, (H - 2) // UNROLL, inner_group, 0)

    for copy, _, receives in halos[2:]:
        @pl.when(receives)
        def _(copy=copy):
            copy.wait_recv()
    for s in range(S):
        first[s, 0] = row_halo[0, s]
        first[s, H + 1] = row_halo[1, s]

    for row in (0, H - 1):
        inner(row)

    for copy, _, receives in halos[:2]:
        @pl.when(receives)
        def _(copy=copy):
            copy.wait_recv()

    def outer(row, target):
        total = [part[row, i] for i in range(3)]
        word, shift = lax.rem(row, HALF), lax.div(row, HALF) * 16
        front, back = ((depth_halo[i, word] >> shift) & 255 for i in range(2))
        for at, grad in (
            (4, first[1, row + 1] - front),
            (10, back - first[S - 2, row + 1]),
        ):
            grad = grad.astype(F32)
            facing = part[row, at + 1] + LIGHT_DEPTH * grad
            square = part[row, at + 2] + grad * grad
            lit = part[row, at] * (0.3 + jnp.abs(facing) * lax.rsqrt(jnp.maximum(square, 4.0)))
            total = [t + part[row, at + 3 + i] * lit for i, t in enumerate(total)]
        total.append(part[row, 3])
        for i in range(2):
            pair = jnp.concatenate(total[2 * i : 2 * i + 2], axis=0)
            target[pl.ds(16 * i, 16)] = pair.astype(jnp.bfloat16)

    def block(k):
        half = lax.div(k + 1, 2)
        return lax.rem(y + Y // 2 + jnp.where(lax.rem(k, 2) == 1, -half, half), Y)

    def across(at, shift):
        to = lax.rem(x + shift, X)
        return pltpu.make_async_remote_copy(
            src_ref=sent.at[at, to], dst_ref=got.at[at, x], send_sem=sent_sem.at[at, to],
            recv_sem=got_sem.at[at, x], device_id=(y * X + to, r), device_id_type=MESH,
        )

    def onward(at):
        return pltpu.make_async_remote_copy(
            src_ref=joined.at[at], dst_ref=met.at[y], send_sem=joined_sem.at[at],
            recv_sem=met_sem.at[y], device_id=(at * X + x, r), device_id_type=MESH,
        )

    def arrival(at, source):
        return pltpu.make_async_remote_copy(
            src_ref=sent.at[at, source], dst_ref=got.at[at, source],
            send_sem=sent_sem.at[at, source], recv_sem=got_sem.at[at, source],
            device_id=(y * X + source, r), device_id_type=MESH,
        )

    def meeting(at):
        return pltpu.make_async_remote_copy(
            src_ref=joined.at[at], dst_ref=met.at[at], send_sem=joined_sem.at[at],
            recv_sem=met_sem.at[at], device_id=(at * X + x, r), device_id_type=MESH,
        )

    shifts = (2, 1, 3)

    def ship(k, _):
        at = block(k)
        for shift in shifts:
            to = lax.rem(x + shift, X)
            outer(at * X + to, sent.at[at, to])
        for shift in shifts:
            across(at, shift).start()
        outer(at * X + x, got.at[at, x])
        return 0

    @pl.when(hears_across)
    def _():
        pl.semaphore_wait(here_sem, 1)

    lax.fori_loop(0, Y, ship, 0)

    def fold(slabs):
        clear = jnp.ones((SUBS, LANES), F32)
        total = [jnp.zeros((SUBS, LANES), F32)] * 3
        for slab in slabs:
            total = [t + clear * slab[SUBS * i : SUBS * (i + 1)] for i, t in enumerate(total)]
            clear = clear - clear * slab[3 * SUBS :]
        return total + [1.0 - clear]

    def join(at, target):
        for shift in shifts:
            arrival(at, lax.rem(x + shift, X)).wait_recv()
        for i, channel in enumerate(fold([got[at, k].astype(F32) for k in range(X)])):
            target[pl.ds(SUBS * i, SUBS)] = channel

    @pl.when(hears_along)
    def _():
        pl.semaphore_wait(here_sem, 1)

    @pl.when(jnp.logical_not(root))
    def _():
        pl.semaphore_wait(news_sem, 2)

    def pass_on(k, _):
        at = block(k)
        join(at, joined.at[at])
        onward(at).start()
        return 0

    lax.fori_loop(0, Y - 1, pass_on, 0)
    join(y, met.at[y])

    def meet(k, _):
        meeting(block(k)).wait_recv()
        return 0

    lax.fori_loop(0, Y - 1, meet, 0)
    for i, channel in enumerate(fold([met[k] for k in range(Y)])):
        out_ref[i] = channel

    def drain(k, _):
        for shift in shifts:
            across(k, shift).wait_send()

        @pl.when(k != y)
        def _():
            onward(k).wait_send()

        return 0

    lax.fori_loop(0, Y, drain, 0)
    for copy, sends, _ in halos:
        @pl.when(sends)
        def _(copy=copy):
            copy.wait_send()


def body(volume, color_map, alpha_map):
    D, R = lax.axis_size("depth"), lax.axis_size("rows")
    S, H = volume.shape[1], volume.shape[2]
    vmem = pl.BlockSpec(memory_space=pltpu.VMEM)
    image = pl.pallas_call(
        functools.partial(kernel, S, H, D, R),
        out_shape=pltpu.VMEM((4, SUBS, LANES), F32),
        in_specs=[pl.BlockSpec(memory_space=pl.ANY)] * 3,
        out_specs=vmem,
        scratch_shapes=[
            pltpu.VMEM(color_map.shape, jnp.int32),
            pltpu.VMEM((2, LANES), jnp.int32),
            pltpu.VMEM((S, H + 2, SUBS, LANES), jnp.int32),
            pltpu.VMEM((S, H, SUBS, LANES), jnp.int32),
            pltpu.VMEM((2, S, SUBS, LANES), jnp.int32),
            pltpu.VMEM((2, H // 2, SUBS, LANES), jnp.int32),
            pltpu.VMEM((2, H // 2, SUBS, LANES), jnp.int32),
            pltpu.VMEM((H, 16, SUBS, LANES), F32),
            pltpu.VMEM((D // X, X, 4 * SUBS, LANES), jnp.bfloat16),
            pltpu.VMEM((D // X, X, 4 * SUBS, LANES), jnp.bfloat16),
            pltpu.VMEM((D // X, 4 * SUBS, LANES), F32),
            pltpu.VMEM((D // X, 4 * SUBS, LANES), F32),
            pltpu.SemaphoreType.DMA((2,)),
            pltpu.SemaphoreType.DMA((2, SUBS)),
            pltpu.SemaphoreType.DMA((4,)),
            pltpu.SemaphoreType.DMA((4,)),
            pltpu.SemaphoreType.DMA((D // X, X)),
            pltpu.SemaphoreType.DMA((D // X, X)),
            pltpu.SemaphoreType.DMA((D // X,)),
            pltpu.SemaphoreType.DMA((D // X,)),
            pltpu.SemaphoreType.REGULAR,
            pltpu.SemaphoreType.REGULAR,
        ],
        compiler_params=pltpu.CompilerParams(collective_id=0, has_side_effects=True),
        name="render",
    )(volume, color_map, alpha_map.reshape(2, LANES))
    return image.reshape(4, 1, SUBS * LANES)


def solution(mesh):
    in_specs = (P(None, "depth", "rows", None), P(), P())
    out_specs = P(None, ("rows", "depth"), None)
    return jax.shard_map(body, mesh=mesh, in_specs=in_specs, out_specs=out_specs, check_vma=False)
```

```python
import functools

import jax
import jax.numpy as jnp
from jax import lax
from jax.experimental import pallas as pl
from jax.experimental.pallas import tpu as pltpu
from jax.sharding import PartitionSpec as P

LIGHT_DEPTH = 0.336
LIGHT_ROWS = 0.42
LIGHT_COLS = 0.448
OPACITY = 4.0
LANES = 128
SUBS = 8
MESH = pl.DeviceIdType.MESH
F32 = jnp.float32
X = 4
UNROLL = 10


def take(table, index):
    return jnp.take_along_axis(table, index, axis=1, mode="promise_in_bounds")


def kernel(
    slices, height, depth_count, row_count,
    volume, color_map, alpha_map, out_ref,
    color_ref, alpha_ref, first, second, row_halo, depth_edge, depth_halo, part, veil_sent, veil_got, sent, got,
    joined, met,
    table_sem, load_sem, halo_send, halo_recv, edge_send, edge_recv, veil_sent_sem, veil_got_sem, sent_sem, got_sem, joined_sem, met_sem, news_sem, here_sem,
):
    S, H, D, R = slices, height, depth_count, row_count
    d, r = lax.axis_index("depth"), lax.axis_index("rows")

    Y = D // X
    y, x = lax.div(d, X), lax.rem(d, X)
    HALF = H // 2

    def along(step):
        return lax.rem(y + step + Y, Y) * X + x

    barrier = pltpu.get_barrier_semaphore()

    def greet(device):
        pl.semaphore_signal(barrier, inc=1, device_id=device, device_id_type=MESH)

    def greet_if(condition, device):
        @pl.when(condition)
        def _():
            greet(device)

    root = d == 0
    crosses_up, crosses_down = (x == X - 1) & (d < D - 1), (x == 0) & (d > 0)
    greet_if(crosses_up, (d + 1, r))
    greet_if(crosses_down, (d - 1, r))
    greet_if(root, (d + 1, r))

    @pl.when(jnp.logical_not(root))
    def _():
        for k in range(1, X):
            greet((y * X + lax.rem(x + k, X), r))
        for step in (1, -1, 2, -2):
            greet((along(step), r))

    greet_if(r > 0, (d, r - 1))
    greet_if(r < R - 1, (d, r + 1))
    greet_if((x == 0) & (y > 2) & (y < Y - 2), (0, r))
    hears_across = (y == 0) & (x > 1)
    hears_along = (x == 0) & (y > 0)
    beside_root = (x == 0) & ((y == 1) | (y == 2) | (y == Y - 1) | (y == Y - 2))
    n_greet = jnp.where(root, X + Y - 2, X + 3 - (hears_across | beside_root).astype(jnp.int32))
    for condition in (crosses_up, crosses_down, r > 0, r < R - 1):
        n_greet = n_greet + condition.astype(jnp.int32)

    tables = [
        pltpu.make_async_copy(color_map, color_ref, table_sem.at[0]),
        pltpu.make_async_copy(alpha_map, alpha_ref, table_sem.at[1]),
    ]
    loads = []
    for p, buffer in enumerate((first, second)):
        for block in range(SUBS):
            source = volume.at[p, :, :, pl.ds(block * LANES, LANES)]
            target = buffer.at[:, pl.ds(1, H), block, :] if p == 0 else buffer.at[:, :, block, :]
            load = pltpu.make_async_copy(source, target, load_sem.at[p, block])
            load.start()
            loads.append(load)
    for table in tables:
        table.start()

    lane = lax.broadcasted_iota(jnp.int32, (SUBS, LANES), 1)
    sub = lax.broadcasted_iota(jnp.int32, (SUBS, LANES), 0)
    last_lane, first_lane = lane == LANES - 1, lane == 0
    not_last, not_first = (sub < SUBS - 1).astype(F32), (sub > 0).astype(F32)

    def spread(row):
        return jnp.broadcast_to(row, (SUBS, LANES))

    zero = jnp.zeros((SUBS, LANES), jnp.int32)

    @pl.when(d == 0)
    def _():
        for i in range(HALF):
            depth_halo[0, i // X, i % X] = zero

    @pl.when(d == D - 1)
    def _():
        for i in range(HALF):
            depth_halo[1, i // X, i % X] = zero

    @pl.when(r == 0)
    def _():
        for s in range(S):
            row_halo[0, s] = zero

    @pl.when(r == R - 1)
    def _():
        for s in range(S):
            row_halo[1, s] = zero

    for load in loads[:SUBS]:
        load.wait()
    def lookups():
        colors = color_ref[0:1] + color_ref[1:2] * 256 + color_ref[2:3] * 65536
        alphas = alpha_ref[...].astype(F32) * (OPACITY / (255.0 * S * D))
        return (
            spread(colors[:, :LANES]), spread(colors[:, LANES:]),
            spread(alphas[0:1]), spread(alphas[1:2]),
        )

    def inner(row, tables):
        color_low, color_high, alpha_low, alpha_high = tables
        clear = jnp.ones((SUBS, LANES), F32)
        total = [jnp.zeros((SUBS, LANES), F32)] * 3
        value = [first[s, row + 1] for s in range(S)]
        for s in range(S):
            level = second[s, row]
            index = level & 127
            opacity = jnp.where(level >= 128, take(alpha_high, index), take(alpha_low, index))
            index = value[s] & 127
            code = jnp.where(value[s] >= 128, take(color_high, index), take(color_low, index))
            emitted = [(code & 255).astype(F32), ((code >> 8) & 255).astype(F32), (code >> 16).astype(F32)]
            here = value[s].astype(F32)
            right = pltpu.roll(here, LANES - 1, 1)
            left = pltpu.roll(here, 1, 1)
            right = jnp.where(last_lane, pltpu.roll(right, SUBS - 1, 0) * not_last, right)
            left = jnp.where(first_lane, pltpu.roll(left, 1, 0) * not_first, left)
            grad_cols = right - left
            grad_rows = (first[s, row + 2] - first[s, row]).astype(F32)
            facing = LIGHT_ROWS * grad_rows + LIGHT_COLS * grad_cols
            square = grad_rows * grad_rows + grad_cols * grad_cols
            weight = clear * opacity
            clear = clear - weight
            if 0 < s < S - 1:
                grad_depth = (value[s + 1] - value[s - 1]).astype(F32)
                facing = facing + LIGHT_DEPTH * grad_depth
                square = square + grad_depth * grad_depth
                lit = weight * (0.3 + jnp.abs(facing) * lax.rsqrt(jnp.maximum(square, 4.0)))
                total = [t + e * lit for t, e in zip(total, emitted)]
            else:
                for i, x in enumerate([weight, facing, square] + emitted):
                    part[row, (4 if s == 0 else 10) + i] = x
        for i, x in enumerate(total + [1.0 - clear]):
            part[row, i] = x

    def interior():
        for load in tables + loads[SUBS:]:
            load.wait()
        looked_up = lookups()

        def inner_group(i, _):
            for k in range(UNROLL):
                inner(UNROLL * i + 1 + k, looked_up)
            return 0

        lax.fori_loop(0, (H - 2) // UNROLL, inner_group, 0)

    computes_first = (d == 1) | (root & (r > 0))

    @pl.when(computes_first)
    def _():
        interior()

    for i in range(HALF):
        depth_edge[0, i // X, i % X] = first[S - 1, i + 1] + first[S - 1, i + 1 + HALF] * 65536
        depth_edge[1, i // X, i % X] = first[0, i + 1] + first[0, i + 1 + HALF] * 65536
    pl.semaphore_wait(barrier, n_greet)

    def halo(which, source, target, device):
        return pltpu.make_async_remote_copy(
            src_ref=source, dst_ref=target, send_sem=halo_send.at[which],
            recv_sem=halo_recv.at[which], device_id=device, device_id_type=MESH,
        )

    def block(k):
        half = lax.div(k + 1, 2)
        return lax.rem(y + Y // 2 + jnp.where(lax.rem(k, 2) == 1, -half, half), Y)

    def edge(which, chunk, device):
        return pltpu.make_async_remote_copy(
            src_ref=depth_edge.at[which, chunk], dst_ref=depth_halo.at[which, chunk],
            send_sem=edge_send.at[which, chunk], recv_sem=edge_recv.at[which, chunk],
            device_id=device, device_id_type=MESH,
        )

    CHUNKS = Y // 2
    edges = (
        (0, (d + 1, r), d < D - 1, d > 0), (1, (d - 1, r), d > 0, d < D - 1),
    )
    for k in range(CHUNKS):
        for which, device, sends, _ in edges:
            @pl.when(sends)
            def _(k=k, which=which, device=device):
                edge(which, lax.rem(block(k), CHUNKS), device).start()
    below = halo(0, first.at[:, H], row_halo.at[0], (d, r + 1))
    above = halo(1, first.at[:, 1], row_halo.at[1], (d, r - 1))
    halos = ((below, r < R - 1, r > 0), (above, r > 0, r < R - 1))
    for copy, sends, _ in halos:
        @pl.when(sends)
        def _(copy=copy):
            copy.start()

    def tell(semaphore, device):
        pl.semaphore_signal(semaphore, inc=1, device_id=device, device_id_type=MESH)

    @pl.when(root)
    def _():
        for k in range(2, X):
            tell(here_sem, (k, r))
        for k in range(1, Y):
            tell(here_sem, (k * X, r))

    for step in (2, -2):
        @pl.when(jnp.logical_not(root) & (along(step) != 0))
        def _(step=step):
            tell(news_sem, (along(step), r))

    @pl.when((x == 0) & (y == 1))
    def _():
        tell(news_sem, (along(1), r))

    @pl.when((x == 0) & (y == Y - 1))
    def _():
        tell(news_sem, (along(-1), r))

    @pl.when(jnp.logical_not(computes_first))
    def _():
        interior()

    for copy, _, receives in halos:
        @pl.when(receives)
        def _(copy=copy):
            copy.wait_recv()
    for s in range(S):
        first[s, 0] = row_halo[0, s]
        first[s, H + 1] = row_halo[1, s]

    looked_up = lookups()
    for row in (0, H - 1):
        inner(row, looked_up)

    def outer(row):
        total = [part[row, i] for i in range(3)]
        chunk, word = lax.rem(lax.div(row, X), CHUNKS), lax.rem(row, X)
        shift = lax.div(row, HALF) * 16
        front, back = ((depth_halo[i, chunk, word] >> shift) & 255 for i in range(2))
        for at, grad in (
            (4, first[1, row + 1] - front),
            (10, back - first[S - 2, row + 1]),
        ):
            grad = grad.astype(F32)
            facing = part[row, at + 1] + LIGHT_DEPTH * grad
            square = part[row, at + 2] + grad * grad
            lit = part[row, at] * (0.3 + jnp.abs(facing) * lax.rsqrt(jnp.maximum(square, 4.0)))
            total = [t + part[row, at + 3 + i] * lit for i, t in enumerate(total)]
        return [t * (1.0 / 255.0) for t in total]

    def two(first_tile, second_tile):
        return jnp.concatenate([first_tile, second_tile], axis=0).astype(jnp.bfloat16)

    shifts = (2, 1, 3)
    PAIRS = Y // 2

    def swap(source, target, send, recv, peer):
        return pltpu.make_async_remote_copy(
            src_ref=source, dst_ref=target, send_sem=send, recv_sem=recv,
            device_id=(y * X + peer, r), device_id_type=MESH,
        )

    def veil(peer, slot):
        return swap(
            veil_sent.at[peer], veil_got.at[slot], veil_sent_sem.at[peer],
            veil_got_sem.at[slot], peer,
        )

    def across(pair, peer, slot):
        return swap(
            sent.at[pair, peer], got.at[pair, slot], sent_sem.at[pair, peer],
            got_sem.at[pair, slot], peer,
        )

    def along_y(at, slot):
        return pltpu.make_async_remote_copy(
            src_ref=joined.at[at], dst_ref=met.at[slot], send_sem=joined_sem.at[at],
            recv_sem=met_sem.at[slot], device_id=(at * X + x, r), device_id_type=MESH,
        )

    @pl.when(hears_across)
    def _():
        pl.semaphore_wait(here_sem, 1)

    for shift in (*shifts, 0):
        peer = lax.rem(x + shift, X)
        target = veil_sent.at[peer] if shift else veil_got.at[x]
        for j in range(PAIRS):
            near, far = block(2 * j) * X + peer, block(2 * j + 1) * X + peer
            target[j] = two(part[near, 3], part[far, 3])
        if shift:
            veil(peer, x).start()

    def ship(j, _):
        pair = (block(2 * j), block(2 * j + 1))
        for at in pair:
            for which, device, _, receives in edges:
                @pl.when(receives & (j < CHUNKS // 2))
                def _(at=at, which=which, device=device):
                    edge(which, lax.rem(at, CHUNKS), device).wait_recv()

        for shift in (*shifts, 0):
            peer = lax.rem(x + shift, X)
            target = sent.at[j, peer] if shift else got.at[j, x]
            channels = zip(*(outer(at * X + peer) for at in pair))
            for i, channel in enumerate(channels):
                target[pl.ds(2 * SUBS * i, 2 * SUBS)] = two(*channel)
        for shift in shifts:
            across(j, lax.rem(x + shift, X), x).start()
        return 0

    lax.fori_loop(0, PAIRS, ship, 0)

    def fold(slabs):
        clear = jnp.ones((SUBS, LANES), F32)
        total = [jnp.zeros((SUBS, LANES), F32)] * 3
        for *colors, opacity in slabs:
            total = [t + clear * c for t, c in zip(total, colors)]
            clear = clear - clear * opacity
        return total + [1.0 - clear]

    @pl.when(hears_along)
    def _():
        pl.semaphore_wait(here_sem, 1)

    @pl.when(jnp.logical_not(root))
    def _():
        pl.semaphore_wait(news_sem, 2)

    for shift in shifts:
        peer = lax.rem(x + shift, X)
        veil(peer, peer).wait_recv()

    for j in range(PAIRS):
        for shift in shifts:
            peer = lax.rem(x + shift, X)
            across(j, peer, peer).wait_recv()
        colors = [got[j, k].astype(F32) for k in range(X)]
        opacities = [veil_got[k, j].astype(F32) for k in range(X)]
        for half in range(2):
            at = block(2 * j + half)
            last = 2 * j + half == Y - 1
            target = met.at[y] if last else joined.at[at]
            low = SUBS * half
            slabs = [
                [c[low + 2 * SUBS * i : low + 2 * SUBS * i + SUBS] for i in range(3)]
                + [o[low : low + SUBS]]
                for c, o in zip(colors, opacities)
            ]
            for i, channel in enumerate(fold(slabs)):
                target[pl.ds(SUBS * i, SUBS)] = channel
            if not last:
                along_y(at, y).start()

    def meet(k, _):
        at = block(k)
        along_y(at, at).wait_recv()
        return 0

    lax.fori_loop(0, Y - 1, meet, 0)
    rows = [met[k] for k in range(Y)]
    rows = [[m[SUBS * i : SUBS * (i + 1)] for i in range(4)] for m in rows]
    for i, channel in enumerate(fold(rows)):
        out_ref[i] = channel

    for shift in shifts:
        peer = lax.rem(x + shift, X)
        veil(peer, x).wait_send()
        for j in range(PAIRS):
            across(j, peer, x).wait_send()

    def drain(k, _):
        along_y(block(k), y).wait_send()
        return 0

    lax.fori_loop(0, Y - 1, drain, 0)
    for copy, sends, _ in halos:
        @pl.when(sends)
        def _(copy=copy):
            copy.wait_send()
    for which, device, sends, _ in edges:
        @pl.when(sends)
        def _(which=which, device=device):
            for chunk in range(CHUNKS):
                edge(which, chunk, device).wait_send()


def body(volume, color_map, alpha_map):
    D, R = lax.axis_size("depth"), lax.axis_size("rows")
    S, H = volume.shape[1], volume.shape[2]
    vmem = pl.BlockSpec(memory_space=pltpu.VMEM)
    image = pl.pallas_call(
        functools.partial(kernel, S, H, D, R),
        out_shape=pltpu.VMEM((4, SUBS, LANES), F32),
        in_specs=[pl.BlockSpec(memory_space=pl.ANY)] * 3,
        out_specs=vmem,
        scratch_shapes=[
            pltpu.VMEM(color_map.shape, jnp.int32),
            pltpu.VMEM((2, LANES), jnp.int32),
            pltpu.VMEM((S, H + 2, SUBS, LANES), jnp.int32),
            pltpu.VMEM((S, H, SUBS, LANES), jnp.int32),
            pltpu.VMEM((2, S, SUBS, LANES), jnp.int32),
            pltpu.VMEM((2, D // X // 2, X, SUBS, LANES), jnp.int32),
            pltpu.VMEM((2, D // X // 2, X, SUBS, LANES), jnp.int32),
            pltpu.VMEM((H, 16, SUBS, LANES), F32),
            pltpu.VMEM((X, D // X // 2, 2 * SUBS, LANES), jnp.bfloat16),
            pltpu.VMEM((X, D // X // 2, 2 * SUBS, LANES), jnp.bfloat16),
            pltpu.VMEM((D // X // 2, X, 6 * SUBS, LANES), jnp.bfloat16),
            pltpu.VMEM((D // X // 2, X, 6 * SUBS, LANES), jnp.bfloat16),
            pltpu.VMEM((D // X, 4 * SUBS, LANES), F32),
            pltpu.VMEM((D // X, 4 * SUBS, LANES), F32),
            pltpu.SemaphoreType.DMA((2,)),
            pltpu.SemaphoreType.DMA((2, SUBS)),
            pltpu.SemaphoreType.DMA((2,)),
            pltpu.SemaphoreType.DMA((2,)),
            pltpu.SemaphoreType.DMA((2, D // X // 2)),
            pltpu.SemaphoreType.DMA((2, D // X // 2)),
            pltpu.SemaphoreType.DMA((X,)),
            pltpu.SemaphoreType.DMA((X,)),
            pltpu.SemaphoreType.DMA((D // X // 2, X)),
            pltpu.SemaphoreType.DMA((D // X // 2, X)),
            pltpu.SemaphoreType.DMA((D // X,)),
            pltpu.SemaphoreType.DMA((D // X,)),
            pltpu.SemaphoreType.REGULAR,
            pltpu.SemaphoreType.REGULAR,
        ],
        compiler_params=pltpu.CompilerParams(collective_id=0, has_side_effects=True),
        name="render",
    )(volume, color_map, alpha_map.reshape(2, LANES))
    return image.reshape(4, 1, SUBS * LANES)


def solution(mesh):
    in_specs = (P(None, "depth", "rows", None), P(), P())
    out_specs = P(None, ("rows", "depth"), None)
    return jax.shard_map(body, mesh=mesh, in_specs=in_specs, out_specs=out_specs, check_vma=False)
```

```python
import functools

import jax
import jax.numpy as jnp
from jax import lax
from jax.experimental import pallas as pl
from jax.experimental.pallas import tpu as pltpu
from jax.sharding import PartitionSpec as P

LIGHT_DEPTH = 0.336
LIGHT_ROWS = 0.42
LIGHT_COLS = 0.448
OPACITY = 4.0
LANES = 128
SUBS = 8
MESH = pl.DeviceIdType.MESH
F32 = jnp.float32
X = 4
UNROLL = 10


def take(table, index):
    return jnp.take_along_axis(table, index, axis=1, mode="promise_in_bounds")


def kernel(
    slices, height, depth_count, row_count,
    volume, color_map, alpha_map, out_ref,
    color_ref, alpha_ref, first, second, row_halo, depth_edge, depth_halo, part, veil_sent, veil_got, sent, got,
    joined, met,
    table_sem, load_sem, halo_send, halo_recv, edge_send, edge_recv, veil_sent_sem, veil_got_sem, sent_sem, got_sem, joined_sem, met_sem, news_sem, here_sem,
):
    S, H, D, R = slices, height, depth_count, row_count
    d, r = lax.axis_index("depth"), lax.axis_index("rows")

    Y = D // X
    y, x = lax.div(d, X), lax.rem(d, X)
    HALF = H // 2

    def along(step):
        return lax.rem(y + step + Y, Y) * X + x

    barrier = pltpu.get_barrier_semaphore()

    def greet(device):
        pl.semaphore_signal(barrier, inc=1, device_id=device, device_id_type=MESH)

    def greet_if(condition, device):
        @pl.when(condition)
        def _():
            greet(device)

    root = d == 0
    crosses_up, crosses_down = (x == X - 1) & (d < D - 1), (x == 0) & (d > 0)
    greet_if(crosses_up, (d + 1, r))
    greet_if(crosses_down, (d - 1, r))
    greet_if(root, (d + 1, r))

    @pl.when(jnp.logical_not(root))
    def _():
        for k in range(1, X):
            greet((y * X + lax.rem(x + k, X), r))
        for step in (1, -1, 2, -2):
            greet((along(step), r))

    greet_if(r > 0, (d, r - 1))
    greet_if(r < R - 1, (d, r + 1))
    greet_if((x == 0) & (y > 2) & (y < Y - 2), (0, r))
    hears_across = (y == 0) & (x > 1)
    hears_along = (x == 0) & (y > 0)
    beside_root = (x == 0) & ((y == 1) | (y == 2) | (y == Y - 1) | (y == Y - 2))
    n_greet = jnp.where(root, X + Y - 2, X + 3 - (hears_across | beside_root).astype(jnp.int32))
    for condition in (crosses_up, crosses_down, r > 0, r < R - 1):
        n_greet = n_greet + condition.astype(jnp.int32)

    tables = [
        pltpu.make_async_copy(color_map, color_ref, table_sem.at[0]),
        pltpu.make_async_copy(alpha_map, alpha_ref, table_sem.at[1]),
    ]
    loads = []
    for p, buffer in enumerate((first, second)):
        for block in range(SUBS):
            source = volume.at[p, :, :, pl.ds(block * LANES, LANES)]
            target = buffer.at[:, pl.ds(1, H), block, :] if p == 0 else buffer.at[:, :, block, :]
            load = pltpu.make_async_copy(source, target, load_sem.at[p, block])
            load.start()
            loads.append(load)
    for table in tables:
        table.start()

    lane = lax.broadcasted_iota(jnp.int32, (SUBS, LANES), 1)
    sub = lax.broadcasted_iota(jnp.int32, (SUBS, LANES), 0)
    last_lane, first_lane = lane == LANES - 1, lane == 0
    not_last, not_first = (sub < SUBS - 1).astype(F32), (sub > 0).astype(F32)

    def spread(row):
        return jnp.broadcast_to(row, (SUBS, LANES))

    zero = jnp.zeros((SUBS, LANES), jnp.int32)

    @pl.when(d == 0)
    def _():
        for i in range(HALF):
            depth_halo[0, i // X, i % X] = zero

    @pl.when(d == D - 1)
    def _():
        for i in range(HALF):
            depth_halo[1, i // X, i % X] = zero

    @pl.when(r == 0)
    def _():
        for s in range(S):
            row_halo[0, s] = zero

    @pl.when(r == R - 1)
    def _():
        for s in range(S):
            row_halo[1, s] = zero

    for load in loads[:SUBS]:
        load.wait()
    def lookups():
        colors = color_ref[0:1] + color_ref[1:2] * 256 + color_ref[2:3] * 65536
        alphas = alpha_ref[...].astype(F32) * (OPACITY / (255.0 * S * D))
        return (
            spread(colors[:, :LANES]), spread(colors[:, LANES:]),
            spread(alphas[0:1]), spread(alphas[1:2]),
        )

    def inner(row, tables):
        color_low, color_high, alpha_low, alpha_high = tables
        clear = jnp.ones((SUBS, LANES), F32)
        total = [jnp.zeros((SUBS, LANES), F32)] * 3
        value = [first[s, row + 1] for s in range(S)]
        for s in range(S):
            level = second[s, row]
            index = level & 127
            opacity = jnp.where(level >= 128, take(alpha_high, index), take(alpha_low, index))
            index = value[s] & 127
            code = jnp.where(value[s] >= 128, take(color_high, index), take(color_low, index))
            emitted = [(code & 255).astype(F32), ((code >> 8) & 255).astype(F32), (code >> 16).astype(F32)]
            here = value[s].astype(F32)
            right = pltpu.roll(here, LANES - 1, 1)
            left = pltpu.roll(here, 1, 1)
            right = jnp.where(last_lane, pltpu.roll(right, SUBS - 1, 0) * not_last, right)
            left = jnp.where(first_lane, pltpu.roll(left, 1, 0) * not_first, left)
            grad_cols = right - left
            grad_rows = (first[s, row + 2] - first[s, row]).astype(F32)
            facing = LIGHT_ROWS * grad_rows + LIGHT_COLS * grad_cols
            square = grad_rows * grad_rows + grad_cols * grad_cols
            weight = clear * opacity
            clear = clear - weight
            if 0 < s < S - 1:
                grad_depth = (value[s + 1] - value[s - 1]).astype(F32)
                facing = facing + LIGHT_DEPTH * grad_depth
                square = square + grad_depth * grad_depth
                lit = weight * (0.3 + jnp.abs(facing) * lax.rsqrt(jnp.maximum(square, 4.0)))
                total = [t + e * lit for t, e in zip(total, emitted)]
            else:
                for i, x in enumerate([weight, facing, square] + emitted):
                    part[row, (4 if s == 0 else 10) + i] = x
        for i, x in enumerate(total + [1.0 - clear]):
            part[row, i] = x

    def interior():
        for load in tables + loads[SUBS:]:
            load.wait()
        looked_up = lookups()

        def inner_group(i, _):
            for k in range(UNROLL):
                inner(UNROLL * i + 1 + k, looked_up)
            return 0

        lax.fori_loop(0, (H - 2) // UNROLL, inner_group, 0)

    computes_first = (d == 1) | (root & (r > 0))

    @pl.when(computes_first)
    def _():
        interior()

    for i in range(HALF):
        depth_edge[0, i // X, i % X] = first[S - 1, i + 1] + first[S - 1, i + 1 + HALF] * 65536
        depth_edge[1, i // X, i % X] = first[0, i + 1] + first[0, i + 1 + HALF] * 65536
    pl.semaphore_wait(barrier, n_greet)

    def halo(which, source, target, device):
        return pltpu.make_async_remote_copy(
            src_ref=source, dst_ref=target, send_sem=halo_send.at[which],
            recv_sem=halo_recv.at[which], device_id=device, device_id_type=MESH,
        )

    def block(k):
        half = lax.div(k + 1, 2)
        return lax.rem(jnp.where(lax.rem(k, 2) == 1, half, Y - half), Y)

    def edge(which, chunk, device):
        return pltpu.make_async_remote_copy(
            src_ref=depth_edge.at[which, chunk], dst_ref=depth_halo.at[which, chunk],
            send_sem=edge_send.at[which, chunk], recv_sem=edge_recv.at[which, chunk],
            device_id=device, device_id_type=MESH,
        )

    CHUNKS = Y // 2
    edges = (
        (0, (d + 1, r), d < D - 1, d > 0), (1, (d - 1, r), d > 0, d < D - 1),
    )
    for k in range(CHUNKS):
        for which, device, sends, _ in edges:
            @pl.when(sends)
            def _(k=k, which=which, device=device):
                edge(which, lax.rem(block(k), CHUNKS), device).start()
    below = halo(0, first.at[:, H], row_halo.at[0], (d, r + 1))
    above = halo(1, first.at[:, 1], row_halo.at[1], (d, r - 1))
    halos = ((below, r < R - 1, r > 0), (above, r > 0, r < R - 1))
    for copy, sends, _ in halos:
        @pl.when(sends)
        def _(copy=copy):
            copy.start()

    def tell(semaphore, device):
        pl.semaphore_signal(semaphore, inc=1, device_id=device, device_id_type=MESH)

    @pl.when(root)
    def _():
        for k in range(2, X):
            tell(here_sem, (k, r))
        for k in range(1, Y):
            tell(here_sem, (k * X, r))

    for step in (2, -2):
        @pl.when(jnp.logical_not(root) & (along(step) != 0))
        def _(step=step):
            tell(news_sem, (along(step), r))

    @pl.when((x == 0) & (y == 1))
    def _():
        tell(news_sem, (along(1), r))

    @pl.when((x == 0) & (y == Y - 1))
    def _():
        tell(news_sem, (along(-1), r))

    @pl.when(jnp.logical_not(computes_first))
    def _():
        interior()

    for copy, _, receives in halos:
        @pl.when(receives)
        def _(copy=copy):
            copy.wait_recv()
    for s in range(S):
        first[s, 0] = row_halo[0, s]
        first[s, H + 1] = row_halo[1, s]

    looked_up = lookups()
    for row in (0, H - 1):
        inner(row, looked_up)

    def outer(row):
        total = [part[row, i] for i in range(3)]
        chunk, word = lax.rem(lax.div(row, X), CHUNKS), lax.rem(row, X)
        shift = lax.div(row, HALF) * 16
        front, back = ((depth_halo[i, chunk, word] >> shift) & 255 for i in range(2))
        for at, grad in (
            (4, first[1, row + 1] - front),
            (10, back - first[S - 2, row + 1]),
        ):
            grad = grad.astype(F32)
            facing = part[row, at + 1] + LIGHT_DEPTH * grad
            square = part[row, at + 2] + grad * grad
            lit = part[row, at] * (0.3 + jnp.abs(facing) * lax.rsqrt(jnp.maximum(square, 4.0)))
            total = [t + part[row, at + 3 + i] * lit for i, t in enumerate(total)]
        return [t * (1.0 / 255.0) for t in total]

    def two(first_tile, second_tile):
        return jnp.concatenate([first_tile, second_tile], axis=0).astype(jnp.bfloat16)

    shifts = (2, 1, 3)
    PAIRS = Y // 2

    def swap(source, target, send, recv, peer):
        return pltpu.make_async_remote_copy(
            src_ref=source, dst_ref=target, send_sem=send, recv_sem=recv,
            device_id=(y * X + peer, r), device_id_type=MESH,
        )

    def veil(peer, slot):
        return swap(
            veil_sent.at[peer], veil_got.at[slot], veil_sent_sem.at[peer],
            veil_got_sem.at[slot], peer,
        )

    def across(pair, peer, slot):
        return swap(
            sent.at[pair, peer], got.at[pair, slot], sent_sem.at[pair, peer],
            got_sem.at[pair, slot], peer,
        )

    def along_y(at, slot):
        return pltpu.make_async_remote_copy(
            src_ref=joined.at[at], dst_ref=met.at[slot], send_sem=joined_sem.at[at],
            recv_sem=met_sem.at[slot], device_id=(at * X + x, r), device_id_type=MESH,
        )

    @pl.when(hears_across)
    def _():
        pl.semaphore_wait(here_sem, 1)

    for shift in (*shifts, 0):
        peer = lax.rem(x + shift, X)
        target = veil_sent.at[peer] if shift else veil_got.at[x]
        for j in range(PAIRS):
            near, far = block(2 * j) * X + peer, block(2 * j + 1) * X + peer
            target[j] = two(part[near, 3], part[far, 3])
        if shift:
            veil(peer, x).start()

    def ship(j, _):
        pair = (block(2 * j), block(2 * j + 1))
        for at in pair:
            for which, device, _, receives in edges:
                @pl.when(receives & (j < CHUNKS // 2))
                def _(at=at, which=which, device=device):
                    edge(which, lax.rem(at, CHUNKS), device).wait_recv()

        for shift in (*shifts, 0):
            peer = lax.rem(x + shift, X)
            target = sent.at[j, peer] if shift else got.at[j, x]
            channels = zip(*(outer(at * X + peer) for at in pair))
            for i, channel in enumerate(channels):
                target[pl.ds(2 * SUBS * i, 2 * SUBS)] = two(*channel)
        for shift in shifts:
            across(j, lax.rem(x + shift, X), x).start()
        return 0

    lax.fori_loop(0, PAIRS, ship, 0)

    def fold(slabs):
        clear = jnp.ones((SUBS, LANES), F32)
        total = [jnp.zeros((SUBS, LANES), F32)] * 3
        for *colors, opacity in slabs:
            total = [t + clear * c for t, c in zip(total, colors)]
            clear = clear - clear * opacity
        return total + [1.0 - clear]

    @pl.when(hears_along)
    def _():
        pl.semaphore_wait(here_sem, 1)

    @pl.when(jnp.logical_not(root))
    def _():
        pl.semaphore_wait(news_sem, 2)

    for shift in shifts:
        peer = lax.rem(x + shift, X)
        veil(peer, peer).wait_recv()

    bound = 1.01 * (1.0 - (1.0 - OPACITY / (S * D)) ** (S * X))

    def encode(channels):
        codes = [(jnp.sqrt(c * (1.0 / bound)) * 65535.0 + 0.5).astype(jnp.int32) for c in channels]
        return [codes[i] + codes[i + 1] * 65536 for i in (0, 2)]

    def decode(words):
        codes = [c.astype(F32) for w in words for c in (w & 65535, (w >> 16) & 65535)]
        return [c * c * (bound / 65535.0**2) for c in codes]

    for j in range(PAIRS):
        for shift in shifts:
            peer = lax.rem(x + shift, X)
            across(j, peer, peer).wait_recv()
        colors = [got[j, k].astype(F32) for k in range(X)]
        opacities = [veil_got[k, j].astype(F32) for k in range(X)]
        for half in range(2):
            at = block(2 * j + half)
            low = SUBS * half
            slabs = [
                [c[low + 2 * SUBS * i : low + 2 * SUBS * i + SUBS] for i in range(3)]
                + [o[low : low + SUBS]]
                for c, o in zip(colors, opacities)
            ]
            words = encode(fold(slabs))

            @pl.when(at == y)
            def _(words=words):
                for i, word in enumerate(words):
                    met[y, i] = word

            @pl.when(at != y)
            def _(at=at, words=words):
                for i, word in enumerate(words):
                    joined[at, i] = word
                along_y(at, y).start()

    def meet(k, _):
        at = lax.rem(y + k, Y)
        along_y(at, at).wait_recv()
        return 0

    lax.fori_loop(1, Y, meet, 0)
    rows = [decode([met[k, i] for i in range(2)]) for k in range(Y)]
    for i, channel in enumerate(fold(rows)):
        out_ref[i] = channel

    for shift in shifts:
        peer = lax.rem(x + shift, X)
        veil(peer, x).wait_send()
        for j in range(PAIRS):
            across(j, peer, x).wait_send()

    def drain(k, _):
        along_y(lax.rem(y + k, Y), y).wait_send()
        return 0

    lax.fori_loop(1, Y, drain, 0)
    for copy, sends, _ in halos:
        @pl.when(sends)
        def _(copy=copy):
            copy.wait_send()
    for which, device, sends, _ in edges:
        @pl.when(sends)
        def _(which=which, device=device):
            for chunk in range(CHUNKS):
                edge(which, chunk, device).wait_send()


def body(volume, color_map, alpha_map):
    D, R = lax.axis_size("depth"), lax.axis_size("rows")
    S, H = volume.shape[1], volume.shape[2]
    vmem = pl.BlockSpec(memory_space=pltpu.VMEM)
    image = pl.pallas_call(
        functools.partial(kernel, S, H, D, R),
        out_shape=pltpu.VMEM((4, SUBS, LANES), F32),
        in_specs=[pl.BlockSpec(memory_space=pl.ANY)] * 3,
        out_specs=vmem,
        scratch_shapes=[
            pltpu.VMEM(color_map.shape, jnp.int32),
            pltpu.VMEM((2, LANES), jnp.int32),
            pltpu.VMEM((S, H + 2, SUBS, LANES), jnp.int32),
            pltpu.VMEM((S, H, SUBS, LANES), jnp.int32),
            pltpu.VMEM((2, S, SUBS, LANES), jnp.int32),
            pltpu.VMEM((2, D // X // 2, X, SUBS, LANES), jnp.int32),
            pltpu.VMEM((2, D // X // 2, X, SUBS, LANES), jnp.int32),
            pltpu.VMEM((H, 16, SUBS, LANES), F32),
            pltpu.VMEM((X, D // X // 2, 2 * SUBS, LANES), jnp.bfloat16),
            pltpu.VMEM((X, D // X // 2, 2 * SUBS, LANES), jnp.bfloat16),
            pltpu.VMEM((D // X // 2, X, 6 * SUBS, LANES), jnp.bfloat16),
            pltpu.VMEM((D // X // 2, X, 6 * SUBS, LANES), jnp.bfloat16),
            pltpu.VMEM((D // X, 2, SUBS, LANES), jnp.int32),
            pltpu.VMEM((D // X, 2, SUBS, LANES), jnp.int32),
            pltpu.SemaphoreType.DMA((2,)),
            pltpu.SemaphoreType.DMA((2, SUBS)),
            pltpu.SemaphoreType.DMA((2,)),
            pltpu.SemaphoreType.DMA((2,)),
            pltpu.SemaphoreType.DMA((2, D // X // 2)),
            pltpu.SemaphoreType.DMA((2, D // X // 2)),
            pltpu.SemaphoreType.DMA((X,)),
            pltpu.SemaphoreType.DMA((X,)),
            pltpu.SemaphoreType.DMA((D // X // 2, X)),
            pltpu.SemaphoreType.DMA((D // X // 2, X)),
            pltpu.SemaphoreType.DMA((D // X,)),
            pltpu.SemaphoreType.DMA((D // X,)),
            pltpu.SemaphoreType.REGULAR,
            pltpu.SemaphoreType.REGULAR,
        ],
        compiler_params=pltpu.CompilerParams(collective_id=0, has_side_effects=True),
        name="render",
    )(volume, color_map, alpha_map.reshape(2, LANES))
    return image.reshape(4, 1, SUBS * LANES)


def solution(mesh):
    in_specs = (P(None, "depth", "rows", None), P(), P())
    out_specs = P(None, ("rows", "depth"), None)
    return jax.shard_map(body, mesh=mesh, in_specs=in_specs, out_specs=out_specs, check_vma=False)
```

```python
import functools

import jax
import jax.numpy as jnp
from jax import lax
from jax.experimental import pallas as pl
from jax.experimental.pallas import tpu as pltpu
from jax.sharding import PartitionSpec as P

LIGHT_DEPTH = 0.336
LIGHT_ROWS = 0.42
LIGHT_COLS = 0.448
OPACITY = 4.0
LANES = 128
SUBS = 8
MESH = pl.DeviceIdType.MESH
F32 = jnp.float32
X = 4
UNROLL = 10


def take(table, index):
    return jnp.take_along_axis(table, index, axis=1, mode="promise_in_bounds")


def kernel(
    slices, height, depth_count, row_count,
    volume, color_map, alpha_map, out_ref,
    color_ref, alpha_ref, first, second, row_halo, depth_edge, depth_halo, part, veil_sent, veil_got, sent, got,
    joined, met,
    table_sem, load_sem, halo_send, halo_recv, edge_send, edge_recv, veil_sent_sem, veil_got_sem, sent_sem, got_sem, joined_sem, met_sem, news_sem, here_sem,
):
    S, H, D, R = slices, height, depth_count, row_count
    d, r = lax.axis_index("depth"), lax.axis_index("rows")

    Y = D // X
    y, x = lax.div(d, X), lax.rem(d, X)
    HALF = H // 2

    def along(step):
        return lax.rem(y + step + Y, Y) * X + x

    barrier = pltpu.get_barrier_semaphore()

    def greet(device):
        pl.semaphore_signal(barrier, inc=1, device_id=device, device_id_type=MESH)

    def greet_if(condition, device):
        @pl.when(condition)
        def _():
            greet(device)

    root = d == 0
    crosses_up, crosses_down = (x == X - 1) & (d < D - 1), (x == 0) & (d > 0)
    greet_if(crosses_up, (d + 1, r))
    greet_if(crosses_down, (d - 1, r))
    greet_if(root, (d + 1, r))

    @pl.when(jnp.logical_not(root))
    def _():
        for k in range(1, X):
            greet((y * X + lax.rem(x + k, X), r))
        for step in (1, -1, 2, -2):
            greet((along(step), r))

    greet_if(r > 0, (d, r - 1))
    greet_if(r < R - 1, (d, r + 1))
    greet_if((x == 0) & (y > 2) & (y < Y - 2), (0, r))
    hears_across = (y == 0) & (x > 1)
    hears_along = (x == 0) & (y > 0)
    beside_root = (x == 0) & ((y == 1) | (y == 2) | (y == Y - 1) | (y == Y - 2))
    n_greet = jnp.where(root, X + Y - 2, X + 3 - (hears_across | beside_root).astype(jnp.int32))
    for condition in (crosses_up, crosses_down, r > 0, r < R - 1):
        n_greet = n_greet + condition.astype(jnp.int32)

    tables = [
        pltpu.make_async_copy(color_map, color_ref, table_sem.at[0]),
        pltpu.make_async_copy(alpha_map, alpha_ref, table_sem.at[1]),
    ]
    loads = []
    for p, buffer in enumerate((first, second)):
        for block in range(SUBS):
            source = volume.at[p, :, :, pl.ds(block * LANES, LANES)]
            target = buffer.at[:, pl.ds(1, H), block, :] if p == 0 else buffer.at[:, :, block, :]
            load = pltpu.make_async_copy(source, target, load_sem.at[p, block])
            load.start()
            loads.append(load)
    for table in tables:
        table.start()

    lane = lax.broadcasted_iota(jnp.int32, (SUBS, LANES), 1)
    sub = lax.broadcasted_iota(jnp.int32, (SUBS, LANES), 0)
    last_lane, first_lane = lane == LANES - 1, lane == 0
    not_last, not_first = (sub < SUBS - 1).astype(F32), (sub > 0).astype(F32)

    def spread(row):
        return jnp.broadcast_to(row, (SUBS, LANES))

    zero = jnp.zeros((SUBS, LANES), jnp.int32)

    @pl.when(d == 0)
    def _():
        for i in range(HALF):
            depth_halo[0, i // X, i % X] = zero

    @pl.when(d == D - 1)
    def _():
        for i in range(HALF):
            depth_halo[1, i // X, i % X] = zero

    @pl.when(r == 0)
    def _():
        for s in range(S):
            row_halo[0, s] = zero

    @pl.when(r == R - 1)
    def _():
        for s in range(S):
            row_halo[1, s] = zero

    for load in loads[:SUBS]:
        load.wait()
    def lookups():
        colors = color_ref[0:1] + color_ref[1:2] * 256 + color_ref[2:3] * 65536
        alphas = alpha_ref[...].astype(F32) * (OPACITY / (255.0 * S * D))
        return (
            spread(colors[:, :LANES]), spread(colors[:, LANES:]),
            spread(alphas[0:1]), spread(alphas[1:2]),
        )

    def inner(row, tables):
        color_low, color_high, alpha_low, alpha_high = tables
        clear = jnp.ones((SUBS, LANES), F32)
        total = [jnp.zeros((SUBS, LANES), F32)] * 3
        value = [first[s, row + 1] for s in range(S)]
        for s in range(S):
            level = second[s, row]
            index = level & 127
            opacity = jnp.where(level >= 128, take(alpha_high, index), take(alpha_low, index))
            index = value[s] & 127
            code = jnp.where(value[s] >= 128, take(color_high, index), take(color_low, index))
            emitted = [(code & 255).astype(F32), ((code >> 8) & 255).astype(F32), (code >> 16).astype(F32)]
            here = value[s].astype(F32)
            right = pltpu.roll(here, LANES - 1, 1)
            left = pltpu.roll(here, 1, 1)
            right = jnp.where(last_lane, pltpu.roll(right, SUBS - 1, 0) * not_last, right)
            left = jnp.where(first_lane, pltpu.roll(left, 1, 0) * not_first, left)
            grad_cols = right - left
            grad_rows = (first[s, row + 2] - first[s, row]).astype(F32)
            facing = LIGHT_ROWS * grad_rows + LIGHT_COLS * grad_cols
            square = grad_rows * grad_rows + grad_cols * grad_cols
            weight = clear * opacity
            clear = clear - weight
            if 0 < s < S - 1:
                grad_depth = (value[s + 1] - value[s - 1]).astype(F32)
                facing = facing + LIGHT_DEPTH * grad_depth
                square = square + grad_depth * grad_depth
                lit = weight * (0.3 + jnp.abs(facing) * lax.rsqrt(jnp.maximum(square, 4.0)))
                total = [t + e * lit for t, e in zip(total, emitted)]
            else:
                for i, x in enumerate([weight, facing, square] + emitted):
                    part[row, (4 if s == 0 else 10) + i] = x
        for i, x in enumerate(total + [1.0 - clear]):
            part[row, i] = x

    def interior():
        for load in tables + loads[SUBS:]:
            load.wait()
        looked_up = lookups()

        def inner_group(i, _):
            for k in range(UNROLL):
                inner(UNROLL * i + 1 + k, looked_up)
            return 0

        lax.fori_loop(0, (H - 2) // UNROLL, inner_group, 0)

    computes_first = (d == 1) | (root & (r > 0))

    @pl.when(computes_first)
    def _():
        interior()

    for i in range(HALF):
        depth_edge[0, i // X, i % X] = first[S - 1, i + 1] + first[S - 1, i + 1 + HALF] * 65536
        depth_edge[1, i // X, i % X] = first[0, i + 1] + first[0, i + 1 + HALF] * 65536
    pl.semaphore_wait(barrier, n_greet)

    def halo(which, source, target, device):
        return pltpu.make_async_remote_copy(
            src_ref=source, dst_ref=target, send_sem=halo_send.at[which],
            recv_sem=halo_recv.at[which], device_id=device, device_id_type=MESH,
        )

    def block(k):
        half = lax.div(k + 1, 2)
        most = lax.rem(jnp.where(lax.rem(k, 2) == 1, half, Y - half), Y)
        first_row = lax.rem(k + 1, Y)
        for at, k_of in ((4, 0), (1, 1), (3, 2), (2, 3)):
            first_row = jnp.where(k == k_of, at, first_row)
        return jnp.where(y == 0, first_row, most)

    def edge(which, chunk, device):
        return pltpu.make_async_remote_copy(
            src_ref=depth_edge.at[which, chunk], dst_ref=depth_halo.at[which, chunk],
            send_sem=edge_send.at[which, chunk], recv_sem=edge_recv.at[which, chunk],
            device_id=device, device_id_type=MESH,
        )

    CHUNKS = Y // 2
    edges = (
        (0, (d + 1, r), d < D - 1, d > 0), (1, (d - 1, r), d > 0, d < D - 1),
    )
    for k in range(CHUNKS):
        for which, device, sends, _ in edges:
            @pl.when(sends)
            def _(k=k, which=which, device=device):
                edge(which, lax.rem(block(k), CHUNKS), device).start()
    below = halo(0, first.at[:, H], row_halo.at[0], (d, r + 1))
    above = halo(1, first.at[:, 1], row_halo.at[1], (d, r - 1))
    halos = ((below, r < R - 1, r > 0), (above, r > 0, r < R - 1))
    for copy, sends, _ in halos:
        @pl.when(sends)
        def _(copy=copy):
            copy.start()

    def tell(semaphore, device):
        pl.semaphore_signal(semaphore, inc=1, device_id=device, device_id_type=MESH)

    @pl.when(root)
    def _():
        for k in range(2, X):
            tell(here_sem, (k, r))
        for k in range(1, Y):
            tell(here_sem, (k * X, r))

    for step in (2, -2):
        @pl.when(jnp.logical_not(root) & (along(step) != 0))
        def _(step=step):
            tell(news_sem, (along(step), r))

    @pl.when((x == 0) & (y == 1))
    def _():
        tell(news_sem, (along(1), r))

    @pl.when((x == 0) & (y == Y - 1))
    def _():
        tell(news_sem, (along(-1), r))

    @pl.when(jnp.logical_not(computes_first))
    def _():
        interior()

    for copy, _, receives in halos:
        @pl.when(receives)
        def _(copy=copy):
            copy.wait_recv()
    for s in range(S):
        first[s, 0] = row_halo[0, s]
        first[s, H + 1] = row_halo[1, s]

    looked_up = lookups()
    for row in (0, H - 1):
        inner(row, looked_up)

    def outer(row):
        total = [part[row, i] for i in range(3)]
        chunk, word = lax.rem(lax.div(row, X), CHUNKS), lax.rem(row, X)
        shift = lax.div(row, HALF) * 16
        front, back = ((depth_halo[i, chunk, word] >> shift) & 255 for i in range(2))
        for at, grad in (
            (4, first[1, row + 1] - front),
            (10, back - first[S - 2, row + 1]),
        ):
            grad = grad.astype(F32)
            facing = part[row, at + 1] + LIGHT_DEPTH * grad
            square = part[row, at + 2] + grad * grad
            lit = part[row, at] * (0.3 + jnp.abs(facing) * lax.rsqrt(jnp.maximum(square, 4.0)))
            total = [t + part[row, at + 3 + i] * lit for i, t in enumerate(total)]
        return [t * (1.0 / 255.0) for t in total]

    def two(first_tile, second_tile):
        return jnp.concatenate([first_tile, second_tile], axis=0).astype(jnp.bfloat16)

    shifts = (2, 1, 3)
    PAIRS = Y // 2

    def swap(source, target, send, recv, peer):
        return pltpu.make_async_remote_copy(
            src_ref=source, dst_ref=target, send_sem=send, recv_sem=recv,
            device_id=(y * X + peer, r), device_id_type=MESH,
        )

    def veil(peer, slot):
        return swap(
            veil_sent.at[peer], veil_got.at[slot], veil_sent_sem.at[peer],
            veil_got_sem.at[slot], peer,
        )

    def across(pair, peer, slot):
        return swap(
            sent.at[pair, peer], got.at[pair, slot], sent_sem.at[pair, peer],
            got_sem.at[pair, slot], peer,
        )

    def along_y(at, slot):
        return pltpu.make_async_remote_copy(
            src_ref=joined.at[at], dst_ref=met.at[slot], send_sem=joined_sem.at[at],
            recv_sem=met_sem.at[slot], device_id=(at * X + x, r), device_id_type=MESH,
        )

    @pl.when(hears_across)
    def _():
        pl.semaphore_wait(here_sem, 1)

    for shift in (*shifts, 0):
        peer = lax.rem(x + shift, X)
        target = veil_sent.at[peer] if shift else veil_got.at[x]
        for j in range(PAIRS):
            near, far = block(2 * j) * X + peer, block(2 * j + 1) * X + peer
            target[j] = two(part[near, 3], part[far, 3])
        if shift:
            veil(peer, x).start()

    def ship(j, _):
        pair = (block(2 * j), block(2 * j + 1))
        for at in pair:
            for which, device, _, receives in edges:
                @pl.when(receives & (j < CHUNKS // 2))
                def _(at=at, which=which, device=device):
                    edge(which, lax.rem(at, CHUNKS), device).wait_recv()

        for shift in (*shifts, 0):
            peer = lax.rem(x + shift, X)
            target = sent.at[j, peer] if shift else got.at[j, x]
            channels = zip(*(outer(at * X + peer) for at in pair))
            for i, channel in enumerate(channels):
                target[pl.ds(2 * SUBS * i, 2 * SUBS)] = two(*channel)
        for shift in shifts:
            across(j, lax.rem(x + shift, X), x).start()
        return 0

    lax.fori_loop(0, PAIRS, ship, 0)

    def fold(slabs):
        clear = jnp.ones((SUBS, LANES), F32)
        total = [jnp.zeros((SUBS, LANES), F32)] * 3
        for *colors, opacity in slabs:
            total = [t + clear * c for t, c in zip(total, colors)]
            clear = clear - clear * opacity
        return total + [1.0 - clear]

    @pl.when(hears_along)
    def _():
        pl.semaphore_wait(here_sem, 1)

    @pl.when(jnp.logical_not(root))
    def _():
        pl.semaphore_wait(news_sem, 2)

    for shift in shifts:
        peer = lax.rem(x + shift, X)
        veil(peer, peer).wait_recv()

    bound = 1.01 * (1.0 - (1.0 - OPACITY / (S * D)) ** (S * X))

    def encode(channels):
        codes = [(jnp.sqrt(c * (1.0 / bound)) * 65535.0 + 0.5).astype(jnp.int32) for c in channels]
        return [codes[i] + codes[i + 1] * 65536 for i in (0, 2)]

    def decode(words):
        codes = [c.astype(F32) for w in words for c in (w & 65535, (w >> 16) & 65535)]
        return [c * c * (bound / 65535.0**2) for c in codes]

    for j in range(PAIRS):
        for shift in shifts:
            peer = lax.rem(x + shift, X)
            across(j, peer, peer).wait_recv()
        colors = [got[j, k].astype(F32) for k in range(X)]
        opacities = [veil_got[k, j].astype(F32) for k in range(X)]
        for half in range(2):
            at = block(2 * j + half)
            low = SUBS * half
            slabs = [
                [c[low + 2 * SUBS * i : low + 2 * SUBS * i + SUBS] for i in range(3)]
                + [o[low : low + SUBS]]
                for c, o in zip(colors, opacities)
            ]
            words = encode(fold(slabs))

            @pl.when(at == y)
            def _(words=words):
                for i, word in enumerate(words):
                    met[y, i] = word

            @pl.when(at != y)
            def _(at=at, words=words):
                for i, word in enumerate(words):
                    joined[at, i] = word
                along_y(at, y).start()

    def meet(k, _):
        at = lax.rem(y + k, Y)
        along_y(at, at).wait_recv()
        return 0

    lax.fori_loop(1, Y, meet, 0)
    rows = [decode([met[k, i] for i in range(2)]) for k in range(Y)]
    for i, channel in enumerate(fold(rows)):
        out_ref[i] = channel

    for shift in shifts:
        peer = lax.rem(x + shift, X)
        veil(peer, x).wait_send()
        for j in range(PAIRS):
            across(j, peer, x).wait_send()

    def drain(k, _):
        along_y(lax.rem(y + k, Y), y).wait_send()
        return 0

    lax.fori_loop(1, Y, drain, 0)
    for copy, sends, _ in halos:
        @pl.when(sends)
        def _(copy=copy):
            copy.wait_send()
    for which, device, sends, _ in edges:
        @pl.when(sends)
        def _(which=which, device=device):
            for chunk in range(CHUNKS):
                edge(which, chunk, device).wait_send()


def body(volume, color_map, alpha_map):
    D, R = lax.axis_size("depth"), lax.axis_size("rows")
    S, H = volume.shape[1], volume.shape[2]
    vmem = pl.BlockSpec(memory_space=pltpu.VMEM)
    image = pl.pallas_call(
        functools.partial(kernel, S, H, D, R),
        out_shape=pltpu.VMEM((4, SUBS, LANES), F32),
        in_specs=[pl.BlockSpec(memory_space=pl.ANY)] * 3,
        out_specs=vmem,
        scratch_shapes=[
            pltpu.VMEM(color_map.shape, jnp.int32),
            pltpu.VMEM((2, LANES), jnp.int32),
            pltpu.VMEM((S, H + 2, SUBS, LANES), jnp.int32),
            pltpu.VMEM((S, H, SUBS, LANES), jnp.int32),
            pltpu.VMEM((2, S, SUBS, LANES), jnp.int32),
            pltpu.VMEM((2, D // X // 2, X, SUBS, LANES), jnp.int32),
            pltpu.VMEM((2, D // X // 2, X, SUBS, LANES), jnp.int32),
            pltpu.VMEM((H, 16, SUBS, LANES), F32),
            pltpu.VMEM((X, D // X // 2, 2 * SUBS, LANES), jnp.bfloat16),
            pltpu.VMEM((X, D // X // 2, 2 * SUBS, LANES), jnp.bfloat16),
            pltpu.VMEM((D // X // 2, X, 6 * SUBS, LANES), jnp.bfloat16),
            pltpu.VMEM((D // X // 2, X, 6 * SUBS, LANES), jnp.bfloat16),
            pltpu.VMEM((D // X, 2, SUBS, LANES), jnp.int32),
            pltpu.VMEM((D // X, 2, SUBS, LANES), jnp.int32),
            pltpu.SemaphoreType.DMA((2,)),
            pltpu.SemaphoreType.DMA((2, SUBS)),
            pltpu.SemaphoreType.DMA((2,)),
            pltpu.SemaphoreType.DMA((2,)),
            pltpu.SemaphoreType.DMA((2, D // X // 2)),
            pltpu.SemaphoreType.DMA((2, D // X // 2)),
            pltpu.SemaphoreType.DMA((X,)),
            pltpu.SemaphoreType.DMA((X,)),
            pltpu.SemaphoreType.DMA((D // X // 2, X)),
            pltpu.SemaphoreType.DMA((D // X // 2, X)),
            pltpu.SemaphoreType.DMA((D // X,)),
            pltpu.SemaphoreType.DMA((D // X,)),
            pltpu.SemaphoreType.REGULAR,
            pltpu.SemaphoreType.REGULAR,
        ],
        compiler_params=pltpu.CompilerParams(collective_id=0, has_side_effects=True),
        name="render",
    )(volume, color_map, alpha_map.reshape(2, LANES))
    return image.reshape(4, 1, SUBS * LANES)


def solution(mesh):
    in_specs = (P(None, "depth", "rows", None), P(), P())
    out_specs = P(None, ("rows", "depth"), None)
    return jax.shard_map(body, mesh=mesh, in_specs=in_specs, out_specs=out_specs, check_vma=False)
```

```python
import functools

import jax
import jax.numpy as jnp
from jax import lax
from jax.experimental import pallas as pl
from jax.experimental.pallas import tpu as pltpu
from jax.sharding import PartitionSpec as P

LIGHT_DEPTH = 0.336
LIGHT_ROWS = 0.42
LIGHT_COLS = 0.448
OPACITY = 4.0
LANES = 128
SUBS = 8
MESH = pl.DeviceIdType.MESH
F32 = jnp.float32
X = 4
UNROLL = 6


def take(table, index):
    return jnp.take_along_axis(table, index, axis=1, mode="promise_in_bounds")


def kernel(
    slices, height, depth_count, row_count,
    volume, color_map, alpha_map, out_ref,
    color_ref, alpha_ref, first, second, row_halo, depth_edge, depth_halo, part, veil_sent, veil_got, sent, got,
    joined, met,
    table_sem, load_sem, halo_send, halo_recv, edge_send, edge_recv, veil_sent_sem, veil_got_sem, sent_sem, got_sem, joined_sem, met_sem, news_sem, here_sem,
):
    S, H, D, R = slices, height, depth_count, row_count
    d, r = lax.axis_index("depth"), lax.axis_index("rows")

    Y = D // X
    y, x = lax.div(d, X), lax.rem(d, X)
    HALF = H // 2

    def along(step):
        return lax.rem(y + step + Y, Y) * X + x

    barrier = pltpu.get_barrier_semaphore()

    def greet(device):
        pl.semaphore_signal(barrier, inc=1, device_id=device, device_id_type=MESH)

    def greet_if(condition, device):
        @pl.when(condition)
        def _():
            greet(device)

    root = d == 0
    crosses_up, crosses_down = (x == X - 1) & (d < D - 1), (x == 0) & (d > 0)
    greet_if(crosses_up, (d + 1, r))
    greet_if(crosses_down, (d - 1, r))
    greet_if(root, (d + 1, r))

    @pl.when(jnp.logical_not(root))
    def _():
        for k in range(1, X):
            greet((y * X + lax.rem(x + k, X), r))
        for step in (1, -1, 2, -2):
            greet((along(step), r))

    greet_if(r > 0, (d, r - 1))
    greet_if(r < R - 1, (d, r + 1))
    greet_if((x == 0) & (y > 2) & (y < Y - 2), (0, r))
    hears_across = (y == 0) & (x > 1)
    hears_along = (x == 0) & (y > 0)
    beside_root = (x == 0) & ((y == 1) | (y == 2) | (y == Y - 1) | (y == Y - 2))
    n_greet = jnp.where(root, X + Y - 2, X + 3 - (hears_across | beside_root).astype(jnp.int32))
    for condition in (crosses_up, crosses_down, r > 0, r < R - 1):
        n_greet = n_greet + condition.astype(jnp.int32)

    tables = [
        pltpu.make_async_copy(color_map, color_ref, table_sem.at[0]),
        pltpu.make_async_copy(alpha_map, alpha_ref, table_sem.at[1]),
    ]
    loads = []
    for p, buffer in enumerate((first, second)):
        for block in range(SUBS):
            source = volume.at[p, :, :, pl.ds(block * LANES, LANES)]
            target = buffer.at[:, pl.ds(1, H), block, :] if p == 0 else buffer.at[:, :, block, :]
            load = pltpu.make_async_copy(source, target, load_sem.at[p, block])
            load.start()
            loads.append(load)
    for table in tables:
        table.start()

    lane = lax.broadcasted_iota(jnp.int32, (SUBS, LANES), 1)
    sub = lax.broadcasted_iota(jnp.int32, (SUBS, LANES), 0)
    last_lane, first_lane = lane == LANES - 1, lane == 0
    not_last, not_first = (sub < SUBS - 1).astype(F32), (sub > 0).astype(F32)

    def spread(row):
        return jnp.broadcast_to(row, (SUBS, LANES))

    zero = jnp.zeros((SUBS, LANES), jnp.int32)

    @pl.when(d == 0)
    def _():
        for i in range(HALF):
            depth_halo[0, i // X, i % X] = zero

    @pl.when(d == D - 1)
    def _():
        for i in range(HALF):
            depth_halo[1, i // X, i % X] = zero

    @pl.when(r == 0)
    def _():
        for s in range(S):
            row_halo[0, s] = zero

    @pl.when(r == R - 1)
    def _():
        for s in range(S):
            row_halo[1, s] = zero

    for load in loads[:SUBS]:
        load.wait()
    def lookups():
        colors = color_ref[0:1] + color_ref[1:2] * 256 + color_ref[2:3] * 65536
        alphas = alpha_ref[...].astype(F32) * (OPACITY / (255.0 * S * D))
        return (
            spread(colors[:, :LANES]), spread(colors[:, LANES:]),
            spread(alphas[0:1]), spread(alphas[1:2]),
        )

    def inner(row, tables):
        color_low, color_high, alpha_low, alpha_high = tables
        clear = jnp.ones((SUBS, LANES), F32)
        total = [jnp.zeros((SUBS, LANES), F32)] * 3
        value = [first[s, row + 1] for s in range(S)]
        for s in range(S):
            level = second[s, row]
            index = level & 127
            opacity = jnp.where(level >= 128, take(alpha_high, index), take(alpha_low, index))
            index = value[s] & 127
            code = jnp.where(value[s] >= 128, take(color_high, index), take(color_low, index))
            emitted = [(code & 255).astype(F32), ((code >> 8) & 255).astype(F32), (code >> 16).astype(F32)]
            here = value[s].astype(F32)
            right = pltpu.roll(here, LANES - 1, 1)
            left = pltpu.roll(here, 1, 1)
            right = jnp.where(last_lane, pltpu.roll(right, SUBS - 1, 0) * not_last, right)
            left = jnp.where(first_lane, pltpu.roll(left, 1, 0) * not_first, left)
            grad_cols = right - left
            grad_rows = (first[s, row + 2] - first[s, row]).astype(F32)
            facing = LIGHT_ROWS * grad_rows + LIGHT_COLS * grad_cols
            square = grad_rows * grad_rows + grad_cols * grad_cols
            weight = clear * opacity
            clear = clear - weight
            if 0 < s < S - 1:
                grad_depth = (value[s + 1] - value[s - 1]).astype(F32)
                facing = facing + LIGHT_DEPTH * grad_depth
                square = square + grad_depth * grad_depth
                lit = weight * (0.3 + jnp.abs(facing) * lax.rsqrt(jnp.maximum(square, 4.0)))
                total = [t + e * lit for t, e in zip(total, emitted)]
            else:
                for i, x in enumerate([weight, facing, square] + emitted):
                    part[row, (4 if s == 0 else 10) + i] = x
        for i, x in enumerate(total + [1.0 - clear]):
            part[row, i] = x

    def interior():
        for load in tables + loads[SUBS:]:
            load.wait()
        looked_up = lookups()

        def inner_group(i, _):
            for k in range(UNROLL):
                inner(UNROLL * i + 1 + k, looked_up)
            return 0

        lax.fori_loop(0, (H - 2) // UNROLL, inner_group, 0)

    computes_first = (d == 1) | (root & (r > 0))

    @pl.when(computes_first)
    def _():
        interior()

    for i in range(HALF):
        depth_edge[0, i // X, i % X] = first[S - 1, i + 1] + first[S - 1, i + 1 + HALF] * 65536
        depth_edge[1, i // X, i % X] = first[0, i + 1] + first[0, i + 1 + HALF] * 65536
    pl.semaphore_wait(barrier, n_greet)

    def halo(which, source, target, device):
        return pltpu.make_async_remote_copy(
            src_ref=source, dst_ref=target, send_sem=halo_send.at[which],
            recv_sem=halo_recv.at[which], device_id=device, device_id_type=MESH,
        )

    def block(k):
        half = lax.div(k + 1, 2)
        most = lax.rem(jnp.where(lax.rem(k, 2) == 1, half, Y - half), Y)
        first_row = lax.rem(k + 1, Y)
        for at, k_of in ((4, 0), (1, 1), (3, 2), (2, 3)):
            first_row = jnp.where(k == k_of, at, first_row)
        return jnp.where(y == 0, first_row, most)

    def edge(which, chunk, device):
        return pltpu.make_async_remote_copy(
            src_ref=depth_edge.at[which, chunk], dst_ref=depth_halo.at[which, chunk],
            send_sem=edge_send.at[which, chunk], recv_sem=edge_recv.at[which, chunk],
            device_id=device, device_id_type=MESH,
        )

    CHUNKS = Y // 2
    edges = (
        (0, (d + 1, r), d < D - 1, d > 0), (1, (d - 1, r), d > 0, d < D - 1),
    )
    for k in range(CHUNKS):
        for which, device, sends, _ in edges:
            @pl.when(sends)
            def _(k=k, which=which, device=device):
                edge(which, lax.rem(block(k), CHUNKS), device).start()
    below = halo(0, first.at[:, H], row_halo.at[0], (d, r + 1))
    above = halo(1, first.at[:, 1], row_halo.at[1], (d, r - 1))
    halos = ((below, r < R - 1, r > 0), (above, r > 0, r < R - 1))
    for copy, sends, _ in halos:
        @pl.when(sends)
        def _(copy=copy):
            copy.start()

    def tell(semaphore, device):
        pl.semaphore_signal(semaphore, inc=1, device_id=device, device_id_type=MESH)

    @pl.when(root)
    def _():
        for k in range(2, X):
            tell(here_sem, (k, r))
        for k in range(1, Y):
            tell(here_sem, (k * X, r))

    for step in (2, -2):
        @pl.when(jnp.logical_not(root) & (along(step) != 0))
        def _(step=step):
            tell(news_sem, (along(step), r))

    @pl.when((x == 0) & (y == 1))
    def _():
        tell(news_sem, (along(1), r))

    @pl.when((x == 0) & (y == Y - 1))
    def _():
        tell(news_sem, (along(-1), r))

    @pl.when(jnp.logical_not(computes_first))
    def _():
        interior()

    for copy, _, receives in halos:
        @pl.when(receives)
        def _(copy=copy):
            copy.wait_recv()
    for s in range(S):
        first[s, 0] = row_halo[0, s]
        first[s, H + 1] = row_halo[1, s]

    looked_up = lookups()
    for row in (0, H - 1):
        inner(row, looked_up)

    def outer(row):
        total = [part[row, i] for i in range(3)]
        chunk, word = lax.rem(lax.div(row, X), CHUNKS), lax.rem(row, X)
        shift = lax.div(row, HALF) * 16
        front, back = ((depth_halo[i, chunk, word] >> shift) & 255 for i in range(2))
        for at, grad in (
            (4, first[1, row + 1] - front),
            (10, back - first[S - 2, row + 1]),
        ):
            grad = grad.astype(F32)
            facing = part[row, at + 1] + LIGHT_DEPTH * grad
            square = part[row, at + 2] + grad * grad
            lit = part[row, at] * (0.3 + jnp.abs(facing) * lax.rsqrt(jnp.maximum(square, 4.0)))
            total = [t + part[row, at + 3 + i] * lit for i, t in enumerate(total)]
        return [t * (1.0 / 255.0) for t in total]

    def two(first_tile, second_tile):
        return jnp.concatenate([first_tile, second_tile], axis=0).astype(jnp.bfloat16)

    shifts = (2, 1, 3)
    PAIRS = Y // 2

    def swap(source, target, send, recv, peer):
        return pltpu.make_async_remote_copy(
            src_ref=source, dst_ref=target, send_sem=send, recv_sem=recv,
            device_id=(y * X + peer, r), device_id_type=MESH,
        )

    def veil(peer, slot):
        return swap(
            veil_sent.at[peer], veil_got.at[slot], veil_sent_sem.at[peer],
            veil_got_sem.at[slot], peer,
        )

    def across(pair, peer, slot):
        return swap(
            sent.at[pair, peer], got.at[pair, slot], sent_sem.at[pair, peer],
            got_sem.at[pair, slot], peer,
        )

    def along_y(at, slot):
        return pltpu.make_async_remote_copy(
            src_ref=joined.at[at], dst_ref=met.at[slot], send_sem=joined_sem.at[at],
            recv_sem=met_sem.at[slot], device_id=(at * X + x, r), device_id_type=MESH,
        )

    @pl.when(hears_across)
    def _():
        pl.semaphore_wait(here_sem, 1)

    for shift in (*shifts, 0):
        peer = lax.rem(x + shift, X)
        target = veil_sent.at[peer] if shift else veil_got.at[x]
        for j in range(PAIRS):
            near, far = block(2 * j) * X + peer, block(2 * j + 1) * X + peer
            target[j] = two(part[near, 3], part[far, 3])
        if shift:
            veil(peer, x).start()

    def ship(j, _):
        pair = (block(2 * j), block(2 * j + 1))
        for at in pair:
            for which, device, _, receives in edges:
                @pl.when(receives & (j < CHUNKS // 2))
                def _(at=at, which=which, device=device):
                    edge(which, lax.rem(at, CHUNKS), device).wait_recv()

        for shift in (*shifts, 0):
            peer = lax.rem(x + shift, X)
            target = sent.at[j, peer] if shift else got.at[j, x]
            channels = zip(*(outer(at * X + peer) for at in pair))
            for i, channel in enumerate(channels):
                target[pl.ds(2 * SUBS * i, 2 * SUBS)] = two(*channel)
        for shift in shifts:
            across(j, lax.rem(x + shift, X), x).start()
        return 0

    lax.fori_loop(0, PAIRS, ship, 0)

    def fold(slabs):
        clear = jnp.ones((SUBS, LANES), F32)
        total = [jnp.zeros((SUBS, LANES), F32)] * 3
        for *colors, opacity in slabs:
            total = [t + clear * c for t, c in zip(total, colors)]
            clear = clear - clear * opacity
        return total + [1.0 - clear]

    @pl.when(hears_along)
    def _():
        pl.semaphore_wait(here_sem, 1)

    @pl.when(jnp.logical_not(root))
    def _():
        pl.semaphore_wait(news_sem, 2)

    for shift in shifts:
        peer = lax.rem(x + shift, X)
        veil(peer, peer).wait_recv()

    bound = 1.01 * (1.0 - (1.0 - OPACITY / (S * D)) ** (S * X))

    def encode(channels):
        codes = [(jnp.sqrt(c * (1.0 / bound)) * 65535.0 + 0.5).astype(jnp.int32) for c in channels]
        return [codes[i] + codes[i + 1] * 65536 for i in (0, 2)]

    def decode(words):
        codes = [c.astype(F32) for w in words for c in (w & 65535, (w >> 16) & 65535)]
        return [c * c * (bound / 65535.0**2) for c in codes]

    for j in range(PAIRS):
        for shift in shifts:
            peer = lax.rem(x + shift, X)
            across(j, peer, peer).wait_recv()
        colors = [got[j, k].astype(F32) for k in range(X)]
        opacities = [veil_got[k, j].astype(F32) for k in range(X)]
        for half in range(2):
            at = block(2 * j + half)
            low = SUBS * half
            slabs = [
                [c[low + 2 * SUBS * i : low + 2 * SUBS * i + SUBS] for i in range(3)]
                + [o[low : low + SUBS]]
                for c, o in zip(colors, opacities)
            ]
            words = encode(fold(slabs))

            @pl.when(at == y)
            def _(words=words):
                for i, word in enumerate(words):
                    met[y, i] = word

            @pl.when(at != y)
            def _(at=at, words=words):
                for i, word in enumerate(words):
                    joined[at, i] = word
                along_y(at, y).start()

    def meet(k, _):
        at = lax.rem(y + k, Y)
        along_y(at, at).wait_recv()
        return 0

    lax.fori_loop(1, Y, meet, 0)
    rows = [decode([met[k, i] for i in range(2)]) for k in range(Y)]
    for i, channel in enumerate(fold(rows)):
        out_ref[i] = channel

    for shift in shifts:
        peer = lax.rem(x + shift, X)
        veil(peer, x).wait_send()
        for j in range(PAIRS):
            across(j, peer, x).wait_send()

    def drain(k, _):
        along_y(lax.rem(y + k, Y), y).wait_send()
        return 0

    lax.fori_loop(1, Y, drain, 0)
    for copy, sends, _ in halos:
        @pl.when(sends)
        def _(copy=copy):
            copy.wait_send()
    for which, device, sends, _ in edges:
        @pl.when(sends)
        def _(which=which, device=device):
            for chunk in range(CHUNKS):
                edge(which, chunk, device).wait_send()


def body(volume, color_map, alpha_map):
    D, R = lax.axis_size("depth"), lax.axis_size("rows")
    S, H = volume.shape[1], volume.shape[2]
    vmem = pl.BlockSpec(memory_space=pltpu.VMEM)
    image = pl.pallas_call(
        functools.partial(kernel, S, H, D, R),
        out_shape=pltpu.VMEM((4, SUBS, LANES), F32),
        in_specs=[pl.BlockSpec(memory_space=pl.ANY)] * 3,
        out_specs=vmem,
        scratch_shapes=[
            pltpu.VMEM(color_map.shape, jnp.int32),
            pltpu.VMEM((2, LANES), jnp.int32),
            pltpu.VMEM((S, H + 2, SUBS, LANES), jnp.int32),
            pltpu.VMEM((S, H, SUBS, LANES), jnp.int32),
            pltpu.VMEM((2, S, SUBS, LANES), jnp.int32),
            pltpu.VMEM((2, D // X // 2, X, SUBS, LANES), jnp.int32),
            pltpu.VMEM((2, D // X // 2, X, SUBS, LANES), jnp.int32),
            pltpu.VMEM((H, 16, SUBS, LANES), F32),
            pltpu.VMEM((X, D // X // 2, 2 * SUBS, LANES), jnp.bfloat16),
            pltpu.VMEM((X, D // X // 2, 2 * SUBS, LANES), jnp.bfloat16),
            pltpu.VMEM((D // X // 2, X, 6 * SUBS, LANES), jnp.bfloat16),
            pltpu.VMEM((D // X // 2, X, 6 * SUBS, LANES), jnp.bfloat16),
            pltpu.VMEM((D // X, 2, SUBS, LANES), jnp.int32),
            pltpu.VMEM((D // X, 2, SUBS, LANES), jnp.int32),
            pltpu.SemaphoreType.DMA((2,)),
            pltpu.SemaphoreType.DMA((2, SUBS)),
            pltpu.SemaphoreType.DMA((2,)),
            pltpu.SemaphoreType.DMA((2,)),
            pltpu.SemaphoreType.DMA((2, D // X // 2)),
            pltpu.SemaphoreType.DMA((2, D // X // 2)),
            pltpu.SemaphoreType.DMA((X,)),
            pltpu.SemaphoreType.DMA((X,)),
            pltpu.SemaphoreType.DMA((D // X // 2, X)),
            pltpu.SemaphoreType.DMA((D // X // 2, X)),
            pltpu.SemaphoreType.DMA((D // X,)),
            pltpu.SemaphoreType.DMA((D // X,)),
            pltpu.SemaphoreType.REGULAR,
            pltpu.SemaphoreType.REGULAR,
        ],
        compiler_params=pltpu.CompilerParams(collective_id=0, has_side_effects=True),
        name="render",
    )(volume, color_map, alpha_map.reshape(2, LANES))
    return image.reshape(4, 1, SUBS * LANES)


def solution(mesh):
    in_specs = (P(None, "depth", "rows", None), P(), P())
    out_specs = P(None, ("rows", "depth"), None)
    return jax.shard_map(body, mesh=mesh, in_specs=in_specs, out_specs=out_specs, check_vma=False)
```
